512 devices in a mesh: group: 16 (over z), sub: 32 (over y, x, core).
Axes of the slice: x: 4, y: 4, z: 16, core: 2. Of those that a mesh axis runs over, the one named last changes fastest.
Arguments:
- points: float32 [3, 1048576], P(None, ('group', 'sub')), may hold values from 0 to 1
- leaf_basis: bfloat16 [1048576, 64], P(('group', 'sub')), as said below
- inner_transfer: bfloat16 [983040, 64], P(('group', 'sub')), as said below
- device_transfer: float32 [32768, 64], P(('group', 'sub')), as said below
- vectors: bfloat16 [1048576, 384], P(('group', 'sub')), may hold values from -0.75 to 0.75
- near_index: int32 [16384, 12], P(('group', 'sub')), may hold values from 0 to 16383, as said below
- near_count: int32 [16384], P(('group', 'sub')), may hold values from 6 to 12, as said below
- far_index: int32 [16384, 3], P(('group', 'sub')), may hold values from 0 to 16383, as said below
Outputs:
- near_product: bfloat16 [1048576, 384], P(('group', 'sub'))
- coupling: bfloat16 [3145728, 64], P(('group', 'sub'))
- device_factor: float32 [32768, 64], P(('group', 'sub'))
- group_factor: float32 [32768, 64], P(('group', 'sub'))
- root_factor: float32 [32768, 64], P(('group', 'sub'))
The draws below stay inside these ranges and needn't reach their ends.
Inputs may be any that keep to these rules, and one draw needn't show every extreme that they name: Slot 0 of near_index[t] is t; the first near_count[t] slots name distinct leaves of layers t // 4 - 1 to t // 4 + 1, all within 7 of t; the remaining slots hold t. far_index[t] names 3 distinct leaves of the window of 15 consecutive leaves centred on t (moved to lie inside 0 to 16383) whose layers differ from t's by two or more. near_count[t] is at most the number of leaves in layers t // 4 - 1 to t // 4 + 1. `inner_transfer`: each K x K block is the identity plus a full matrix, nonsingular. `device_transfer`: each K x K block is nonsingular. `leaf_basis`: each leaf's block has full column rank.
All inputs are finite; a program needn't handle non-finite values.
Results may differ from the reference program's by a relative error of at most 0.005.
Values may be sent and summed in bfloat16 or wider, within the bound.
A program may use at most 64 MiB of HBM per device.

```python
import jax
import jax.numpy as jnp
from jax import lax

K = 64
P_SIZE = 64
LEAF_DEV = 32
NVEC = 384
LAYER = 4
RAD = 7
NEAR = 12
FAR = 3
NLEAF = 16384
N_GROUP = 16
N_SUB = 32


MIX_WEIGHT = 0.85


def near_lists(key):
    window = 2 * RAD + 1
    key_order, key_count, key_place, key_far = jax.random.split(jax.random.fold_in(key, 7), 4)
    leaf_ids = jnp.arange(NLEAF, dtype=jnp.int32)
    lowest = jnp.clip(leaf_ids - RAD, 0, NLEAF - window)
    columns = jnp.arange(window, dtype=jnp.int32)
    candidates = (lowest[:, None] + columns[None, :]).astype(jnp.int32)
    layer_gap = jnp.abs(candidates // LAYER - leaf_ids[:, None] // LAYER)
    adjacent = layer_gap <= 1
    is_self = candidates == leaf_ids[:, None]
    large_score = (1 << 16) * window + window
    near_scores = jax.random.randint(key_order, (NLEAF, window), 0, 1 << 16, dtype=jnp.int32) * window + columns[None, :]
    near_scores = jnp.where(adjacent, near_scores, large_score + columns[None, :])
    near_scores = jnp.where(is_self, -1, near_scores)
    near_order = jnp.argsort(near_scores, axis=1).astype(jnp.int32)
    near_listed = jnp.take_along_axis(candidates, near_order, axis=1)
    far_scores = jax.random.randint(key_far, (NLEAF, window), 0, 1 << 16, dtype=jnp.int32) * window + columns[None, :]
    far_scores = jnp.where(adjacent, large_score + columns[None, :], far_scores)
    far_order = jnp.argsort(far_scores, axis=1).astype(jnp.int32)
    far_listed = jnp.take_along_axis(candidates, far_order[:, :FAR], axis=1).astype(jnp.int32)
    adjacent_count = jnp.sum(adjacent.astype(jnp.int32), axis=1)
    counts = jax.random.randint(key_count, (NLEAF,), NEAR // 2, NEAR + 1, dtype=jnp.int32)
    chosen = jax.random.randint(key_place, (), LAYER, NLEAF - LAYER, dtype=jnp.int32)
    counts = jnp.where(leaf_ids == chosen, NEAR, counts)
    counts = jnp.minimum(counts, adjacent_count).astype(jnp.int32)
    slots = jnp.arange(NEAR, dtype=jnp.int32)
    near = jnp.where(slots[None, :] < counts[:, None], near_listed[:, :NEAR], leaf_ids[:, None]).astype(jnp.int32)
    return (near, counts, far_listed)


def draw_near_index(key, part):
    return near_lists(key)[0]


def draw_near_count(key, part):
    return near_lists(key)[1]


def draw_far_index(key, part):
    return near_lists(key)[2]


def noise_block(key, shape, fan_in, spread):
    values = jax.random.normal(key, shape, jnp.float32)
    return values * (spread / fan_in ** 0.5)


def column_mixing(values):
    return values + MIX_WEIGHT * jnp.roll(values, 1, axis=1)


def draw_leaf_basis(key, part):
    row_ids = jnp.arange(NLEAF * P_SIZE, dtype=jnp.int32)
    col_ids = jnp.arange(K, dtype=jnp.int32)
    identity = ((row_ids % P_SIZE)[:, None] == col_ids[None, :]).astype(jnp.float32)
    values = 1.5 * identity + noise_block(key, (NLEAF * P_SIZE, K), P_SIZE, 0.5)
    return column_mixing(values).astype(jnp.bfloat16)


def draw_inner_transfer(key, part):
    total_rows = N_GROUP * N_SUB * (LEAF_DEV - 2) * K
    row_ids = jnp.arange(total_rows, dtype=jnp.int32)
    col_ids = jnp.arange(K, dtype=jnp.int32)
    identity = ((row_ids % K)[:, None] == col_ids[None, :]).astype(jnp.float32)
    values = identity + noise_block(key, (total_rows, K), K, 0.35)
    return values.astype(jnp.bfloat16)


def draw_device_transfer(key, part):
    devices = N_GROUP * N_SUB
    key_noise = jax.random.fold_in(key, 0)
    row_ids = jnp.arange(devices * K, dtype=jnp.int32)
    col_ids = jnp.arange(K, dtype=jnp.int32)
    identity = ((row_ids % K)[:, None] == col_ids[None, :]).astype(jnp.float32)
    device_ids = (row_ids // K).astype(jnp.float32)
    rising = jnp.sqrt(1.0 + 2.0 * device_ids / (devices - 1))
    values = (identity + noise_block(key_noise, (devices * K, K), K, 0.35)) * rising[:, None]
    return column_mixing(values).astype(jnp.float32)


def level_of(key, extent, cuts, low, largest):
    loudness = 1.0
    for axis_at, shards_of in cuts:
        heights = jax.random.uniform(jax.random.fold_in(jax.random.fold_in(key, 6), axis_at), (shards_of,), jnp.float32, low / len(cuts), largest / len(cuts))
        loudness = loudness * jnp.repeat(jnp.exp(heights), extent[axis_at] // shards_of).reshape((-1,) + (1,) * (len(extent) - 1 - axis_at))
    return loudness


def noise(key, dims, scale, reach, cuts=(), kind=jnp.bfloat16):
    factor_of = level_of(key, dims, cuts, -0.22, 0.18) if cuts else 1.0
    values = jax.random.normal(key, dims, jnp.float32) * scale * factor_of
    return jnp.minimum(jnp.maximum(values, -reach), reach).astype(kind)


def setup_inputs(seed: int = 0) -> dict:
    arg_keys = jax.random.split(jax.random.key(seed), 9)
    points = jnp.clip(1.0 * jax.random.uniform(arg_keys[0], (3, NLEAF * P_SIZE), jnp.float32) ** level_of(arg_keys[0], (3, NLEAF * P_SIZE), ((1, 512),), -0.2, 0.2), 0.0, 1.0)
    leaf_basis = draw_leaf_basis(jax.random.fold_in(arg_keys[8], 71), 0)
    inner_transfer = draw_inner_transfer(jax.random.fold_in(arg_keys[8], 71), 0)
    device_transfer = draw_device_transfer(jax.random.fold_in(arg_keys[8], 71), 0)
    vectors = noise(arg_keys[4], (NLEAF * P_SIZE, NVEC), 0.125, 0.75, ((0, 512),))
    near_index = draw_near_index(jax.random.fold_in(arg_keys[8], 71), 0)
    near_count = draw_near_count(jax.random.fold_in(arg_keys[8], 71), 0)
    far_index = draw_far_index(jax.random.fold_in(arg_keys[8], 71), 0)
    return dict(points=points, leaf_basis=leaf_basis, inner_transfer=inner_transfer, device_transfer=device_transfer, vectors=vectors, near_index=near_index, near_count=near_count, far_index=far_index)


SHORT_SQ = 0.09
LONG_SQ = 2.25
LONG_WEIGHT = 0.5

def gram_matrix(matrix):
    return jnp.einsum('...ik,...il->...kl', matrix, matrix, precision=lax.Precision.HIGHEST)

def upper_factor(gram):
    return jnp.swapaxes(jnp.linalg.cholesky(gram), -1, -2)

def product(left_side, right_side):
    return jnp.einsum('...ij,...jk->...ik', left_side, right_side, precision=lax.Precision.HIGHEST)

def local_tree(leaf_factor, inner_blocks):
    factor = leaf_factor
    node_count = leaf_factor.shape[-3]
    levels = node_count.bit_length() - 1
    offset = 0
    for level in range(levels):
        merged = (gram_matrix(factor[..., 0::2, :, :]) + gram_matrix(factor[..., 1::2, :, :])) * 0.5
        factor = upper_factor(merged)
        node_count = node_count // 2
        if level + 1 < levels:
            factor = product(factor, inner_blocks[..., offset:offset + node_count, :, :])
            offset = offset + node_count
    return factor[..., 0, :, :]

def cell_offset(target, source):
    across = target % 2 - source % 2
    along = target // 2 % 2 - source // 2 % 2
    layer_gap = target // LAYER - source // LAYER
    return jnp.stack([across, along, layer_gap], axis=-1).astype(jnp.float32)

def leaf_kernel(first_pts, second_pts, offsets):
    differences = first_pts[..., :, :, None] - second_pts[..., :, None, :] + offsets[..., :, None, None]
    distance = jnp.sum(differences * differences, axis=-3)
    return jnp.exp(distance * (-0.5 / SHORT_SQ)) + LONG_WEIGHT * jnp.exp(distance * (-0.5 / LONG_SQ))

def reference(points, leaf_basis, inner_transfer, device_transfer, vectors, near_index, near_count, far_index):
    devices = N_GROUP * N_SUB
    basis_full = leaf_basis.astype(jnp.float32).reshape(NLEAF, P_SIZE, K)
    leaf_factor = upper_factor(gram_matrix(basis_full))
    inner_blocks = inner_transfer.astype(jnp.float32).reshape(devices, LEAF_DEV - 2, K, K)
    subtree_top = local_tree(leaf_factor.reshape(devices, LEAF_DEV, K, K), inner_blocks)
    device_factor = product(subtree_top, device_transfer.reshape(devices, K, K))
    grouped = device_factor.reshape(N_GROUP, N_SUB, K, K)
    group_factor = upper_factor(jnp.mean(gram_matrix(grouped), axis=1))
    root_factor = upper_factor(jnp.mean(gram_matrix(group_factor), axis=0))
    group_copies = jnp.repeat(group_factor, N_SUB, axis=0).reshape(devices * K, K)
    root_copies = jnp.broadcast_to(root_factor[None], (devices, K, K)).reshape(devices * K, K)
    coords = points.reshape(3, NLEAF, P_SIZE).transpose(1, 0, 2)
    blocks = vectors.reshape(NLEAF, P_SIZE, NVEC)

    def one_block(block_start):
        target = block_start + jnp.arange(LEAF_DEV, dtype=jnp.int32)
        near_rows = lax.dynamic_slice_in_dim(near_index, block_start, LEAF_DEV, 0)
        count_rows = lax.dynamic_slice_in_dim(near_count, block_start, LEAF_DEV, 0)
        far_rows = lax.dynamic_slice_in_dim(far_index, block_start, LEAF_DEV, 0)
        own_pts = jnp.take(coords, target, axis=0)
        running = jnp.zeros((LEAF_DEV, P_SIZE, NVEC), jnp.float32)
        for slot_index in range(NEAR):
            source = near_rows[:, slot_index]
            weights = leaf_kernel(own_pts, jnp.take(coords, source, axis=0), cell_offset(target, source))
            weights = jnp.where((slot_index < count_rows)[:, None, None], weights, 0.0).astype(jnp.bfloat16)
            gathered = jnp.take(blocks, source, axis=0)
            running = running + jnp.einsum('lij,ljv->liv', weights.astype(jnp.float32), gathered.astype(jnp.float32), precision=lax.Precision.HIGHEST)
        own_factor = jnp.take(leaf_factor, target, axis=0)
        pieces = []
        for slot_index in range(FAR):
            source = far_rows[:, slot_index]
            kernel_block = leaf_kernel(own_pts, jnp.take(coords, source, axis=0), cell_offset(target, source))
            other_factor = jnp.take(leaf_factor, source, axis=0)
            projected = product(product(own_factor, kernel_block), jnp.swapaxes(other_factor, -1, -2)) / K
            pieces.append(projected)
        return (running.astype(jnp.bfloat16), jnp.stack(pieces, axis=1).astype(jnp.bfloat16))
    starts = jnp.arange(NLEAF // LEAF_DEV, dtype=jnp.int32) * LEAF_DEV
    near_out, coupling_out = lax.map(one_block, starts)
    near_product = near_out.reshape(NLEAF * P_SIZE, NVEC)
    coupling = coupling_out.reshape(NLEAF * FAR * K, K)
    return (near_product, coupling, device_factor.reshape(devices * K, K), group_copies, root_copies)
```

```python
import functools
import math

import jax
import jax.numpy as jnp
from jax import lax
from jax.experimental import pallas as pl
from jax.experimental.pallas import tpu as pltpu
from jax.sharding import PartitionSpec as P

K = 64
LAYER = 4
HALO = 8
OWN = 32
WIDE = OWN + 2 * HALO
SHORT_SQ = 0.09
LONG_SQ = 2.25
RATIO = LONG_SQ / SHORT_SQ
SCALE = math.sqrt(0.5 / LONG_SQ * math.log2(math.e))
OFF = -1.0e5
VMEM_LIMIT = 48 << 20
F32 = jnp.float32
BF16 = jnp.bfloat16


def shifted(block, axis, distance):
    devices = range(lax.axis_size(axis))
    route = [(i - distance, i) for i in devices if i - distance in devices]
    return lax.ppermute(block, axis, route)


def dot(a, b):
    return jnp.dot(a, b, preferred_element_type=F32)


def dot_t(a, b):
    return lax.dot_general(a, b, (((0,), (0,)), ((), ())), preferred_element_type=F32)


def dot_nt(a, b):
    return lax.dot_general(a, b, (((1,), (1,)), ((), ())), preferred_element_type=F32)


def exact_dot(a, b):
    return jnp.dot(a, b, preferred_element_type=F32, precision=lax.Precision.HIGHEST)


def exact_dot_t(a, b):
    return lax.dot_general(
        a, b, (((0,), (0,)), ((), ())), preferred_element_type=F32, precision=lax.Precision.HIGHEST
    )


def split3(x):
    high = x.astype(BF16)
    rest = x - high.astype(F32)
    middle = rest.astype(BF16)
    low = (rest - middle.astype(F32)).astype(BF16)
    return high, middle, low


def split2(x):
    high = x.astype(BF16)
    return high, (x - high.astype(F32)).astype(BF16)


def wide_dot(exact, x):
    high, middle, low = split3(x)
    return dot(exact, high) + (dot(exact, middle) + dot(exact, low))


def cholesky_rows(a_ref):
    lanes = a_ref.shape[2]
    for block in range(K // 4):
        first = 4 * block
        start = first // 8 * 8
        rows = tuple(a_ref[first + q, start:K, :] for q in range(4))

        def subtract(k, rows):
            done = a_ref[k, start:K, :]
            return tuple(
                rows[q] - a_ref[k, first + q : first + q + 1, :] * done for q in range(4)
            )

        if first:
            rows = lax.fori_loop(0, first, subtract, rows, unroll=4)
        rows = list(rows)
        index = lax.broadcasted_iota(jnp.int32, (K - start, lanes), 0)
        for q in range(4):
            at = first + q - start
            row = rows[q] * lax.rsqrt(rows[q][at : at + 1, :])
            row = jnp.where(index >= at, row, 0.0)
            a_ref[first + q, start:K, :] = row
            if start:
                a_ref[first + q, 0:start, :] = jnp.zeros((start, lanes), F32)
            for other in range(q + 1, 4):
                into = first + other - start
                rows[other] = rows[other] - row[into : into + 1, :] * row


def tree_kernel(basis_ref, inner_ref, transfer_ref, leaf_ref, factor_ref, gram_ref, g_ref, a_ref):
    slots = a_ref.shape[2]
    path = [inner_ref[(28 + m) * K : (29 + m) * K, :].astype(F32) for m in range(2)]
    for first, count in ((24, 4), (16, 8), (0, 16)):
        longer = []
        for m in range(count // 2):
            rows = inner_ref[(first + 2 * m) * K : (first + 2 * m + 2) * K, :]
            both = wide_dot(rows, path[m])
            longer += [both[:K], both[K:]]
        path = longer
    top = jnp.zeros((K, K), F32)
    for m in range(16):
        x = wide_dot(basis_ref[2 * m * K : (2 * m + 2) * K, :], path[m])
        top = top + exact_dot_t(x, x)
    top = top * (1.0 / OWN)
    transfer = transfer_ref[...]
    gram_ref[...] = exact_dot_t(transfer, exact_dot(top, transfer))
    for t in range(OWN):
        v = basis_ref[t * K : (t + 1) * K, :]
        g_ref[t * K : (t + 1) * K, :] = dot_t(v, v)
    for t in range(OWN, slots):
        g_ref[t * K : (t + 1) * K, :] = top
    for i in range(K):
        a_ref[i] = g_ref[pl.ds(i, slots, stride=K), :].T
    cholesky_rows(a_ref)
    for i in range(K):
        g_ref[pl.ds(i, slots, stride=K), :] = a_ref[i].T
    leaf_ref[...] = g_ref[0 : OWN * K, :]
    factor_ref[...] = exact_dot(g_ref[OWN * K : (OWN + 1) * K, :], transfer)


def tree_call(leaf_basis, inner_transfer, device_transfer):
    slots = 40
    whole = pl.BlockSpec(memory_space=pltpu.VMEM)
    return pl.pallas_call(
        tree_kernel,
        out_shape=(
            jax.ShapeDtypeStruct((OWN * K, K), F32),
            jax.ShapeDtypeStruct((K, K), F32),
            jax.ShapeDtypeStruct((K, K), F32),
        ),
        in_specs=[whole] * 3,
        out_specs=(whole,) * 3,
        scratch_shapes=[
            pltpu.VMEM((slots * K, K), F32),
            pltpu.VMEM((K, K, slots), F32),
        ],
        compiler_params=pltpu.CompilerParams(vmem_limit_bytes=VMEM_LIMIT),
    )(leaf_basis, inner_transfer, device_transfer)


def final_kernel(group_ref, root_ref, group_out, root_out, a_ref):
    for i in range(K):
        lane = lax.broadcasted_iota(jnp.int32, (K, 128), 1)
        a_ref[i] = jnp.where(lane < 64, group_ref[:, i : i + 1], root_ref[:, i : i + 1])
    cholesky_rows(a_ref)
    lane = lax.broadcasted_iota(jnp.int32, (K, 128), 1)
    group_t = jnp.zeros((K, 128), F32)
    root_t = jnp.zeros((K, 128), F32)
    for i in range(K):
        row = a_ref[i]
        group_t = jnp.where(lane == i, row, group_t)
        root_t = jnp.where(lane == i + 64, row, root_t)
    group_out[...] = group_t.T[:K, :]
    root_out[...] = root_t.T[K:, :]


def final_call(group_gram, root_gram):
    whole = pl.BlockSpec(memory_space=pltpu.VMEM)
    return pl.pallas_call(
        final_kernel,
        out_shape=(jax.ShapeDtypeStruct((K, K), F32),) * 2,
        in_specs=[whole] * 2,
        out_specs=(whole,) * 2,
        scratch_shapes=[pltpu.VMEM((K, K, 128), F32)],
        compiler_params=pltpu.CompilerParams(vmem_limit_bytes=VMEM_LIMIT),
    )(group_gram, root_gram)


def kernel_values(exponent):
    return jnp.exp2(exponent * RATIO) + 0.5 * jnp.exp2(exponent)


def field_kernel(
    coords_ref,
    near_ref,
    count_ref,
    far_ref,
    left_ref,
    own_ref,
    right_ref,
    factor_ref,
    near_out,
    coupling_out,
    source_ref,
    target_ref,
    leaf_source_ref,
    index_ref,
    off_ref,
    factor_high,
    factor_low,
    block_ref,
    half_ref,
):
    first_leaf = (lax.axis_index("group") * lax.axis_size("sub") + lax.axis_index("sub")) * OWN
    lanes = WIDE * K
    leaf = lax.broadcasted_iota(jnp.int32, (1, lanes), 1) // K
    corners = (leaf % 2, leaf // 2 % 2, leaf // LAYER - WIDE // LAYER // 2)
    ones = jnp.ones((1, lanes), F32)
    target_rows, source_rows, norm = [], [], jnp.zeros((1, lanes), F32)
    for c in range(3):
        u = (coords_ref[c : c + 1, :] + corners[c].astype(F32)) * SCALE
        high, middle, low = (part.astype(F32) for part in split3(u))
        norm = norm - u * u
        for a, b in (
            (high, high),
            (high, middle),
            (middle, high),
            (high, low),
            (low, high),
            (middle, middle),
        ):
            target_rows.append(2.0 * a)
            source_rows.append(b)
    for part in split3(norm):
        target_rows += [part.astype(F32), ones]
        source_rows += [ones, part.astype(F32)]
    for p in range(LAYER):
        target_rows.append((leaf % LAYER == p).astype(F32))
        source_rows.append(jnp.zeros((1, lanes), F32))
    for _ in range(4):
        target_rows.append(jnp.zeros((1, lanes), F32))
        source_rows.append(jnp.zeros((1, lanes), F32))
    for r in range(32):
        source_ref[r : r + 1, :] = source_rows[r]
    for r in range(32):
        target_rows[r] = target_rows[r][:, HALO * K : (HALO + OWN) * K]
    targets = jnp.concatenate(target_rows, axis=0)
    target_ref[...] = targets.T.astype(BF16)
    for w in range(WIDE):
        leaf_source_ref[w] = source_ref[:, w * K : (w + 1) * K].astype(BF16)

    slot = lax.broadcasted_iota(jnp.int32, (8, 128), 1)
    row = lax.broadcasted_iota(jnp.int32, (8, 128), 0)
    for layer in range(OWN // LAYER):
        index_ref[...] = jnp.full((8, 128), -1, jnp.int32)
        index_ref[0:LAYER, 0:12] = near_ref[LAYER * layer : LAYER * (layer + 1), :]
        used = jnp.zeros((8, 128), jnp.int32)
        for p in range(LAYER):
            used = jnp.where(row == p, count_ref[LAYER * layer + p], used)
        place = index_ref[...] - (first_leaf + LAYER * (layer - 1))
        place = jnp.where(slot < used, place, -1)
        present = jnp.zeros((8, 128), jnp.bool_)
        for n in range(12):
            present = present | (place[:, n : n + 1] == slot)
        bias = jnp.where(present | (row >= LAYER), 0.0, OFF)
        for pair in range(6):
            off_ref[layer, :, pair * 128 : (pair + 1) * 128] = jnp.where(
                slot < K, bias[:, 2 * pair : 2 * pair + 1], bias[:, 2 * pair + 1 : 2 * pair + 2]
            )

    def vectors(layer):
        if layer < 0:
            return left_ref[...]
        if layer >= OWN // LAYER:
            return right_ref[...]
        return own_ref[layer * LAYER * K : (layer + 1) * LAYER * K, :]

    width = LAYER * K
    for layer in range(OWN // LAYER):
        total = jnp.zeros((width, own_ref.shape[1]), F32)
        for step in range(3):
            at = (layer + 1 + step) * width
            source = jnp.concatenate(
                [
                    source_ref[0:24, at : at + width],
                    source_ref[24:32, at : at + width]
                    + off_ref[layer, :, step * width : (step + 1) * width],
                ],
                axis=0,
            ).astype(BF16)
            exponent = dot(target_ref[layer * width : (layer + 1) * width, :], source)
            weights = kernel_values(exponent).astype(BF16)
            total = total + dot(weights, vectors(layer - 1 + step))
        near_out[layer * width : (layer + 1) * width, :] = total.astype(BF16)

    for w in range(WIDE):
        high, low = split2(factor_ref[w * K : (w + 1) * K, :])
        factor_high[w] = high
        factor_low[w] = low

    def blocks(pair, _):
        t = pair // 3
        w = far_ref[t, pair - 3 * t] - first_leaf + HALO
        exponent = dot(target_ref[pl.ds(t * K, K), :], leaf_source_ref[w])
        high, low = split2(kernel_values(exponent))
        block_ref[pair, 0] = high
        block_ref[pair, 1] = low
        return 0

    lax.fori_loop(0, 3 * OWN, blocks, 0, unroll=4)

    def halves(pair, _):
        t = pair // 3
        high, low = factor_high[t + HALO], factor_low[t + HALO]
        s_high, s_low = block_ref[pair, 0], block_ref[pair, 1]
        half = dot(high, s_high) + (dot(high, s_low) + dot(low, s_high))
        half_high, half_low = split2(half * (1.0 / K))
        half_ref[pair, 0] = half_high
        half_ref[pair, 1] = half_low
        return 0

    lax.fori_loop(0, 3 * OWN, halves, 0, unroll=4)

    def projected(pair, _):
        t = pair // 3
        w = far_ref[t, pair - 3 * t] - first_leaf + HALO
        high, low = factor_high[w], factor_low[w]
        h_high, h_low = half_ref[pair, 0], half_ref[pair, 1]
        value = dot_nt(h_high, high) + (dot_nt(h_high, low) + dot_nt(h_low, high))
        coupling_out[pl.ds(pair * K, K), :] = value.astype(BF16)
        return 0

    lax.fori_loop(0, 3 * OWN, projected, 0, unroll=4)


def field_call(coords, near_index, near_count, far_index, left, own, right, factors):
    whole = pl.BlockSpec(memory_space=pltpu.VMEM)
    scalars = pl.BlockSpec(memory_space=pltpu.SMEM)
    return pl.pallas_call(
        field_kernel,
        out_shape=(
            jax.ShapeDtypeStruct(own.shape, BF16),
            jax.ShapeDtypeStruct((3 * OWN * K, K), BF16),
        ),
        in_specs=[whole, whole, scalars, scalars, whole, whole, whole, whole],
        out_specs=(whole, whole),
        scratch_shapes=[
            pltpu.VMEM((32, WIDE * K), F32),
            pltpu.VMEM((OWN * K, 32), BF16),
            pltpu.VMEM((WIDE, 32, K), BF16),
            pltpu.VMEM((8, 128), jnp.int32),
            pltpu.VMEM((OWN // LAYER, 8, 12 * K), F32),
            pltpu.VMEM((WIDE, K, K), BF16),
            pltpu.VMEM((WIDE, K, K), BF16),
            pltpu.VMEM((3 * OWN, 2, K, K), BF16),
            pltpu.VMEM((3 * OWN, 2, K, K), BF16),
        ],
        compiler_params=pltpu.CompilerParams(vmem_limit_bytes=VMEM_LIMIT),
    )(coords, near_index, near_count, far_index, left, own, right, factors)


def per_device(
    points, leaf_basis, inner_transfer, device_transfer, vectors, near_index, near_count, far_index
):
    both = ("group", "sub")
    edge = HALO * K
    left_vectors = shifted(vectors[-LAYER * K :], both, 1)
    right_vectors = shifted(vectors[: LAYER * K], both, -1)
    left_points = shifted(points[:, -edge:], both, 1)
    right_points = shifted(points[:, :edge], both, -1)
    leaf_factor, device_factor, device_gram = tree_call(leaf_basis, inner_transfer, device_transfer)
    left_factor = shifted(leaf_factor[-edge:], both, 1)
    right_factor = shifted(leaf_factor[:edge], both, -1)
    group_gram = lax.psum(device_gram, "sub") * (1.0 / lax.axis_size("sub"))
    root_gram = lax.psum(group_gram, "group") * (1.0 / lax.axis_size("group"))
    coords = jnp.concatenate([left_points, points, right_points], axis=1)
    factors = jnp.concatenate([left_factor, leaf_factor, right_factor], axis=0)
    near_product, coupling = field_call(
        coords, near_index, near_count, far_index, left_vectors, vectors, right_vectors, factors
    )
    group_factor, root_factor = final_call(group_gram, root_gram)
    return near_product, coupling, device_factor, group_factor, root_factor


def solution(mesh):
    rows = P(("group", "sub"), None)
    return jax.shard_map(
        per_device,
        mesh=mesh,
        in_specs=(
            P(None, ("group", "sub")),
            rows,
            rows,
            rows,
            rows,
            rows,
            P(("group", "sub")),
            rows,
        ),
        out_specs=(rows,) * 5,
        check_vma=False,
    )
```

```python
import math

import jax
import jax.numpy as jnp
from jax import lax
from jax.experimental import pallas as pl
from jax.experimental.pallas import tpu as pltpu
from jax.sharding import PartitionSpec as P

K = 64
PAIR = 2 * K
LAYER = 4
NEAR = 12
FAR = 3
HALO = 8
OWN = 32
WIDE = OWN + 2 * HALO
EDGE = HALO * K
SLOTS = 40
SHORT_SQ = 0.09
LONG_SQ = 2.25
RATIO = LONG_SQ / SHORT_SQ
SCALE = math.sqrt(0.5 / LONG_SQ * math.log2(math.e))
OFF = -131072.0
VMEM_LIMIT = 48 << 20
F32 = jnp.float32
BF16 = jnp.bfloat16
MESH = pl.DeviceIdType.MESH
ROUNDS = 5
SENT = 13


def dot(a, b):
    return jnp.dot(a, b, preferred_element_type=F32)


def dot_nt(a, b):
    return lax.dot_general(a, b, (((1,), (1,)), ((), ())), preferred_element_type=F32)


def exact_dot(a, b):
    return jnp.dot(a, b, preferred_element_type=F32, precision=lax.Precision.HIGHEST)


def exact_dot_t(a, b):
    return lax.dot_general(
        a, b, (((0,), (0,)), ((), ())), preferred_element_type=F32, precision=lax.Precision.HIGHEST
    )


def split3(x):
    high = x.astype(BF16)
    rest = x - high.astype(F32)
    middle = rest.astype(BF16)
    low = (rest - middle.astype(F32)).astype(BF16)
    return high, middle, low


def dot_wide(x, exact):
    rows = x.shape[0]
    parts = dot(jnp.concatenate(split3(x), axis=0), exact)
    return parts[:rows] + (parts[rows : 2 * rows] + parts[2 * rows :])


def in_first_half(shape):
    return lax.broadcasted_iota(jnp.int32, shape, len(shape) - 1) < K


def high_low(doubled):
    high = doubled.astype(BF16).astype(F32)
    return jnp.where(in_first_half(doubled.shape), high, doubled - high).astype(BF16)


def add_halves(x):
    return x + pltpu.roll(x, K, axis=1)


def cholesky_rows(a_ref, blocks):
    lanes = a_ref.shape[2]
    for block in blocks:
        first = 4 * block
        start = first // 8 * 8
        rows = tuple(a_ref[first + q, start:K, :] for q in range(4))

        def subtract(k, rows):
            done = a_ref[k, start:K, :]
            return tuple(
                rows[q] - a_ref[k, first + q : first + q + 1, :] * done for q in range(4)
            )

        if first:
            rows = lax.fori_loop(0, first, subtract, rows, unroll=4)
        rows = list(rows)
        index = lax.broadcasted_iota(jnp.int32, (K - start, lanes), 0)
        for q in range(4):
            at = first + q - start
            row = rows[q] * lax.rsqrt(rows[q][at : at + 1, :])
            row = jnp.where(index >= at, row, 0.0)
            a_ref[first + q, start:K, :] = row
            if start:
                a_ref[first + q, 0:start, :] = jnp.zeros((start, lanes), F32)
            for other in range(q + 1, 4):
                into = first + other - start
                rows[other] = rows[other] - row[into : into + 1, :] * row


def tree_gram(basis_ref, inner_ref, x_ref):
    last = inner_ref[:, 14 * PAIR : 15 * PAIR].astype(F32)
    path = [last[:, :K], last[:, K:]]
    for first, count in ((12, 4), (8, 8), (0, 16)):
        longer = []
        for m in range(count // 2):
            both = dot_wide(path[m], inner_ref[:, (first + m) * PAIR : (first + m + 1) * PAIR])
            longer += [both[:, :K], both[:, K:]]
        path = longer
    for m in range(16):
        x = dot_wide(path[m], basis_ref[:, m * PAIR : (m + 1) * PAIR])
        for part, value in enumerate(split3(x)):
            x_ref[part * K : (part + 1) * K, m * PAIR : (m + 1) * PAIR] = value
    parts = dot_nt(x_ref[0:PAIR, :], x_ref[...])
    parts = parts[:K] + parts[K:]
    low = parts[:, PAIR : PAIR + K]
    return (parts[:, :K] + parts[:, K:PAIR] + (low + low.T)) * (1.0 / OWN)


def unpack(ref):
    return jnp.concatenate([ref[:, :K], ref[:, K:]], axis=0)


def upsweep_kernel(
    basis_ref,
    inner_ref,
    transfer_ref,
    points_ref,
    vectors_ref,
    factor_out,
    group_out,
    root_out,
    pairs_out,
    own_pairs_out,
    left_points,
    right_points,
    left_vectors,
    right_vectors,
    g_ref,
    d_ref,
    a_ref,
    last_ref,
    x_ref,
    sum_ref,
    got_ref,
    send_sem,
    recv_sem,
):
    groups, subs = lax.axis_size("group"), lax.axis_size("sub")
    g, s = lax.axis_index("group"), lax.axis_index("sub")
    me = g * subs + s
    after = lax.rem(me + 1, groups * subs)
    before = lax.rem(me + groups * subs - 1, groups * subs)
    after = (after // subs, lax.rem(after, subs))
    before = (before // subs, lax.rem(before, subs))

    def turned(index, stride, size, by):
        at = lax.rem(index // stride, size)
        return index + (lax.rem(at + by, size) - at) * stride

    rounds = [
        [(g, turned(s, 1, 2, 1))],
        [(g, turned(s, 2, 4, by)) for by in (1, 2, 3)],
        [(g, turned(s, 8, 4, by)) for by in (1, 2, 3)],
        [(turned(g, 1, 4, by), s) for by in (1, 2, 3)],
        [(turned(g, 4, 4, by), s) for by in (1, 2, 3)],
    ]
    offsets = [0, 1, 4, 7, 10]

    barrier = pltpu.get_barrier_semaphore()
    greeted = [after, before] + [device for stage in rounds for device in stage]
    for device in greeted:
        pl.semaphore_signal(barrier, inc=1, device_id=device, device_id_type=MESH)
    pl.semaphore_wait(barrier, len(greeted))

    def copy(number, source, target, device):
        return pltpu.make_async_remote_copy(
            src_ref=source,
            dst_ref=target,
            send_sem=send_sem.at[number],
            recv_sem=recv_sem.at[number],
            device_id=device,
            device_id_type=MESH,
        )

    rows, lanes = vectors_ref.shape[0], points_ref.shape[1]
    halos = [
        copy(SENT, vectors_ref.at[rows - LAYER * K : rows], left_vectors, after),
        copy(SENT + 1, vectors_ref.at[0 : LAYER * K], right_vectors, before),
        copy(SENT + 2, points_ref.at[:, lanes - EDGE : lanes], left_points, after),
        copy(SENT + 3, points_ref.at[:, 0:EDGE], right_points, before),
    ]
    for halo in halos:
        halo.start()

    def send(stage):
        copies = [
            copy(offsets[stage] + n, sum_ref.at[stage], got_ref.at[offsets[stage] + n], device)
            for n, device in enumerate(rounds[stage])
        ]
        for one in copies:
            one.start()
        return copies

    def receive(stage, copies):
        total = sum_ref[stage]
        for n, one in enumerate(copies):
            one.wait()
            total = total + got_ref[offsets[stage] + n]
        sum_ref[stage + 1] = total

    top = tree_gram(basis_ref, inner_ref, x_ref)
    transfer = transfer_ref[...]
    gram = exact_dot_t(transfer, exact_dot(top, transfer))
    sum_ref[0] = jnp.concatenate([gram[: K // 2], gram[K // 2 :]], axis=1)
    sent = send(0)

    first = in_first_half((K, PAIR))
    for m in range(OWN // 2):
        v = basis_ref[:, m * PAIR : (m + 1) * PAIR]
        zero = jnp.zeros_like(v)
        one_each = jnp.concatenate([jnp.where(first, v, zero), jnp.where(first, zero, v)], axis=0)
        g_ref[m * PAIR : (m + 1) * PAIR, :] = dot_nt(one_each, v)
    for t in range(OWN, SLOTS):
        g_ref[t * K : (t + 1) * K, :] = top
    receive(0, sent)
    sent = send(1)
    for i in range(K):
        a_ref[i] = g_ref[pl.ds(i, SLOTS, stride=K), :].T
    receive(1, sent)
    sent = send(2)
    cholesky_rows(a_ref, range(0, 7))
    receive(2, sent)
    sent = send(3)
    cholesky_rows(a_ref, range(7, 16))
    receive(3, sent)
    sent = send(4)
    for i in range(K):
        row = a_ref[i]
        d_ref[pl.ds(i, SLOTS, stride=K), :] = jnp.concatenate([row, row], axis=0).T
    for t in range(OWN):
        doubled = d_ref[t * K : (t + 1) * K, :]
        high = doubled.astype(BF16).astype(F32)
        low = doubled - high
        pair = jnp.where(first, high, low).astype(BF16)
        pairs_out[EDGE + t * K : EDGE + (t + 1) * K, :] = pair
        own_pairs_out[t * PAIR : t * PAIR + K, :] = pair
        own_pairs_out[t * PAIR + K : (t + 1) * PAIR, :] = jnp.where(first, low, high).astype(BF16)
    edges = [
        copy(SENT + 4, pairs_out.at[OWN * K : OWN * K + EDGE], pairs_out.at[0:EDGE], after),
        copy(
            SENT + 5,
            pairs_out.at[EDGE : 2 * EDGE],
            pairs_out.at[OWN * K + EDGE : OWN * K + 2 * EDGE],
            before,
        ),
    ]
    for edge in edges:
        edge.start()
    factor_out[...] = exact_dot(d_ref[OWN * K : (OWN + 1) * K, 0:K], transfer)
    receive(4, sent)

    group = unpack(sum_ref[3]) * (1.0 / subs)
    root = unpack(sum_ref[5]) * (1.0 / (subs * groups))
    for i in range(K):
        last_ref[i] = jnp.where(first, group[:, i : i + 1], root[:, i : i + 1])
    cholesky_rows(last_ref, range(16))
    lane = lax.broadcasted_iota(jnp.int32, (K, PAIR), 1)
    columns = jnp.zeros((K, PAIR), F32)
    others = jnp.zeros((K, PAIR), F32)
    for i in range(K):
        row = last_ref[i]
        columns = jnp.where(lane == i, row, columns)
        others = jnp.where(lane == i + K, row, others)
    group_out[...] = columns.T[:K, :]
    root_out[...] = others.T[K:, :]
    for done in halos + edges:
        done.wait()


def upsweep_call(basis_t, inner_t, transfer, points, vectors):
    whole = pl.BlockSpec(memory_space=pltpu.VMEM)
    anywhere = pl.BlockSpec(memory_space=pl.ANY)
    square = jax.ShapeDtypeStruct((K, K), F32)
    edge_points = jax.ShapeDtypeStruct((points.shape[0], EDGE), F32)
    edge_vectors = jax.ShapeDtypeStruct((LAYER * K, vectors.shape[1]), BF16)
    copies = SENT + 6
    return pl.pallas_call(
        upsweep_kernel,
        out_shape=(
            square,
            square,
            square,
            jax.ShapeDtypeStruct((WIDE * K, PAIR), BF16),
            jax.ShapeDtypeStruct((OWN * PAIR, PAIR), BF16),
            edge_points,
            edge_points,
            edge_vectors,
            edge_vectors,
        ),
        in_specs=[whole] * 4 + [anywhere],
        out_specs=(whole,) * 7 + (anywhere,) * 2,
        scratch_shapes=[
            pltpu.VMEM((SLOTS * K, K), F32),
            pltpu.VMEM((SLOTS * K, PAIR), F32),
            pltpu.VMEM((K, K, SLOTS), F32),
            pltpu.VMEM((K, K, PAIR), F32),
            pltpu.VMEM((3 * K, OWN * K), BF16),
            pltpu.VMEM((ROUNDS + 1, K // 2, PAIR), F32),
            pltpu.VMEM((SENT, K // 2, PAIR), F32),
            pltpu.SemaphoreType.DMA((copies,)),
            pltpu.SemaphoreType.DMA((copies,)),
        ],
        compiler_params=pltpu.CompilerParams(
            collective_id=0, has_side_effects=True, vmem_limit_bytes=VMEM_LIMIT
        ),
    )(basis_t, inner_t, transfer, points, vectors)


def kernel_values(exponent):
    return jnp.exp2(exponent * RATIO) + 0.5 * jnp.exp2(exponent)


def field_kernel(
    left_points,
    points_ref,
    right_points,
    near_ref,
    count_ref,
    far_ref,
    left_ref,
    own_ref,
    right_ref,
    pairs_ref,
    own_pairs_ref,
    factor_ref,
    group_ref,
    root_ref,
    near_out,
    coupling_out,
    factor_out,
    group_out,
    root_out,
    coords_ref,
    source_ref,
    target_ref,
    source_t_ref,
    target_t_ref,
    doubled_ref,
    block_ref,
    half_ref,
):
    factor_out[...] = factor_ref[...]
    group_out[...] = group_ref[...]
    root_out[...] = root_ref[...]
    first_leaf = (lax.axis_index("group") * lax.axis_size("sub") + lax.axis_index("sub")) * OWN
    lanes = WIDE * K
    coords_ref[:, 0:EDGE] = left_points[...]
    coords_ref[:, EDGE : lanes - EDGE] = points_ref[...]
    coords_ref[:, lanes - EDGE : lanes] = right_points[...]
    leaf = lax.broadcasted_iota(jnp.int32, (3, lanes), 1) // K
    axis = lax.broadcasted_iota(jnp.int32, (3, lanes), 0)
    corner = jnp.where(
        axis == 0, leaf % 2, jnp.where(axis == 1, leaf // 2 % 2, leaf // LAYER - WIDE // LAYER // 2)
    )
    u = (coords_ref[...] + corner.astype(F32)) * SCALE
    high, middle, low = (part.astype(F32) for part in split3(u))
    norms = [part.astype(F32) for part in split3(-jnp.sum(u * u, axis=0, keepdims=True))]
    ones = jnp.ones((3, lanes), F32)
    own = slice(EDGE, lanes - EDGE)
    for n, (a, b) in enumerate(
        (
            (high, high),
            (high, middle),
            (middle, high),
            (high, low),
            (low, high),
            (middle, middle),
        )
    ):
        target_ref[3 * n : 3 * n + 3, :] = 2.0 * a[:, own]
        source_ref[3 * n : 3 * n + 3, :] = b
    target_ref[18:21, :] = ones[:, own]
    source_ref[21:24, :] = ones
    for n, part in enumerate(norms):
        source_ref[18 + n : 19 + n, :] = part
        target_ref[21 + n : 22 + n, :] = part[:, own]
    source_ref[24:32, :] = jnp.zeros((8, lanes), F32)

    slot = lax.broadcasted_iota(jnp.int32, (NEAR, OWN), 0)
    target = lax.broadcasted_iota(jnp.int32, (NEAR, OWN), 1)
    used = jnp.zeros((NEAR, OWN), jnp.int32)
    for t in range(OWN):
        used = jnp.where(target == t, count_ref[t], used)
    place = near_ref[...] - (first_leaf - LAYER) - target // LAYER * LAYER
    place = jnp.where(slot < used, place, -1)
    window = lax.broadcasted_iota(jnp.int32, (16, OWN), 0)
    bias = jnp.full((16, OWN), OFF, F32)
    for n in range(NEAR):
        bias = jnp.where(place[n : n + 1, :] == window, 0.0, bias)
    spread = lax.broadcasted_iota(jnp.int32, (OWN, OWN * K), 1) // K
    spread = (spread == lax.broadcasted_iota(jnp.int32, (OWN, OWN * K), 0)).astype(F32)
    target_ref[24:40, :] = dot(bias.astype(BF16), spread.astype(BF16))

    target_t_ref[...] = target_ref[...].T.astype(BF16)
    source_t_ref[...] = source_ref[...].T.astype(BF16)
    for t in range(OWN):
        one = target_ref[0:32, t * K : (t + 1) * K]
        doubled_ref[t] = jnp.concatenate([one, one], axis=1).astype(BF16)

    def vectors(layer):
        if layer < 0:
            return left_ref[...]
        if layer >= OWN // LAYER:
            return right_ref[...]
        return own_ref[layer * LAYER * K : (layer + 1) * LAYER * K, :]

    width = LAYER * K
    window = lax.broadcasted_iota(jnp.int32, (16, width), 0)
    column = lax.broadcasted_iota(jnp.int32, (16, width), 1) // K
    for layer in range(OWN // LAYER):
        total = jnp.zeros((width, own_ref.shape[1]), F32)
        for step in range(3):
            at = (layer + 1 + step) * width
            place = (window == column + LAYER * step).astype(F32)
            source = jnp.concatenate([source_ref[0:24, at : at + width], place], axis=0)
            exponent = dot(
                target_t_ref[layer * width : (layer + 1) * width, :], source.astype(BF16)
            )
            weights = kernel_values(exponent).astype(BF16)
            total = total + dot(weights, vectors(layer - 1 + step))
        near_out[layer * width : (layer + 1) * width, :] = total.astype(BF16)

    def leaf_rows(ref, leaf, rows):
        return ref[pl.ds(pl.multiple_of(leaf * rows, rows), rows), :]

    def blocks(t, _):
        sources = [
            leaf_rows(source_t_ref, far_ref[f, t] - first_leaf + HALO, K) for f in range(FAR)
        ]
        exponent = dot(jnp.concatenate(sources, axis=0), doubled_ref[t])
        block_ref[t] = high_low(kernel_values(exponent))
        return 0

    lax.fori_loop(0, OWN, blocks, 0, unroll=4)

    def halves(t, _):
        value = dot_nt(block_ref[t], leaf_rows(own_pairs_ref, t, PAIR))
        half_ref[t] = high_low(add_halves(value) * (1.0 / K))
        return 0

    lax.fori_loop(0, OWN, halves, 0, unroll=4)

    def projected(pair, _):
        values = []
        for t in (2 * pair, 2 * pair + 1):
            for f in range(FAR):
                half = half_ref[t, f * K : (f + 1) * K, :]
                pairs = leaf_rows(pairs_ref, far_ref[f, t] - first_leaf + HALO, K)
                values.append(add_halves(dot(pairs, jnp.concatenate([half, half], axis=0))))
        first = in_first_half((K, PAIR))
        both = [jnp.where(first, values[2 * n], values[2 * n + 1]) for n in range(FAR)]
        at = pl.multiple_of(pair * FAR * PAIR, PAIR)
        coupling_out[:, pl.ds(at, FAR * PAIR)] = jnp.concatenate(both, axis=1).astype(BF16)
        return 0

    lax.fori_loop(0, OWN // 2, projected, 0, unroll=2)


def field_call(left, points, right, near_t, near_count, far_t, *rest):
    whole = pl.BlockSpec(memory_space=pltpu.VMEM)
    scalars = pl.BlockSpec(memory_space=pltpu.SMEM)
    vectors = rest[1]
    square = jax.ShapeDtypeStruct((K, K), F32)
    return pl.pallas_call(
        field_kernel,
        out_shape=(
            jax.ShapeDtypeStruct(vectors.shape, BF16),
            jax.ShapeDtypeStruct((K, FAR * OWN * K), BF16),
            square,
            square,
            square,
        ),
        in_specs=[whole] * 4 + [scalars] * 2 + [whole] * len(rest),
        out_specs=(whole,) * 5,
        scratch_shapes=[
            pltpu.VMEM((3, WIDE * K), F32),
            pltpu.VMEM((32, WIDE * K), F32),
            pltpu.VMEM((40, OWN * K), F32),
            pltpu.VMEM((WIDE * K, 32), BF16),
            pltpu.VMEM((OWN * K, 40), BF16),
            pltpu.VMEM((OWN, 32, PAIR), BF16),
            pltpu.VMEM((OWN, FAR * K, PAIR), BF16),
            pltpu.VMEM((OWN, FAR * K, PAIR), BF16),
        ],
        compiler_params=pltpu.CompilerParams(vmem_limit_bytes=VMEM_LIMIT),
    )(left, points, right, near_t, near_count, far_t, *rest)


def per_device(
    points, leaf_basis, inner_transfer, device_transfer, vectors, near_index, near_count, far_index
):
    factor, group, root, pairs, own_pairs, left_points, right_points, left, right = upsweep_call(
        leaf_basis.T, inner_transfer.T, device_transfer, points, vectors
    )
    near_product, coupling_t, device_factor, group_factor, root_factor = field_call(
        left_points,
        points,
        right_points,
        near_index.T,
        near_count,
        far_index.T,
        left,
        vectors,
        right,
        pairs,
        own_pairs,
        factor,
        group,
        root,
    )
    return near_product, coupling_t.T, device_factor, group_factor, root_factor


def solution(mesh):
    rows = P(("group", "sub"), None)
    return jax.shard_map(
        per_device,
        mesh=mesh,
        in_specs=(
            P(None, ("group", "sub")),
            rows,
            rows,
            rows,
            rows,
            rows,
            P(("group", "sub")),
            rows,
        ),
        out_specs=(rows,) * 5,
        check_vma=False,
    )
```

```python
import math

import jax
import jax.numpy as jnp
from jax import lax
from jax.experimental import pallas as pl
from jax.experimental.pallas import tpu as pltpu
from jax.sharding import PartitionSpec as P

K = 64
PAIR = 2 * K
LAYER = 4
RAD = 7
NEAR = 12
FAR = 3
HALO = 8
OWN = 32
WIDE = OWN + 2 * HALO
EDGE = HALO * K
SLOTS = 40
SHORT_SQ = 0.09
LONG_SQ = 2.25
RATIO = LONG_SQ / SHORT_SQ
SCALE = math.sqrt(0.5 / LONG_SQ * math.log2(math.e))
OFF = -131072.0
VMEM_LIMIT = 60 << 20
F32 = jnp.float32
BF16 = jnp.bfloat16
MESH = pl.DeviceIdType.MESH
PLANE = 15
WINDOW = 7
COVER = 4
SUMS = PLANE + WINDOW + COVER
COPIES = SUMS + 6
INPUTS = 6
FIRST_PART = 10


def dot(a, b):
    return jnp.dot(a, b, preferred_element_type=F32)


def dot_nt(a, b):
    return lax.dot_general(a, b, (((1,), (1,)), ((), ())), preferred_element_type=F32)


def exact_dot(a, b):
    return jnp.dot(a, b, preferred_element_type=F32, precision=lax.Precision.HIGHEST)


def exact_dot_t(a, b):
    return lax.dot_general(
        a, b, (((0,), (0,)), ((), ())), preferred_element_type=F32, precision=lax.Precision.HIGHEST
    )


def split3(x):
    high = x.astype(BF16)
    rest = x - high.astype(F32)
    middle = rest.astype(BF16)
    low = (rest - middle.astype(F32)).astype(BF16)
    return high, middle, low


def dot_wide(x, exact):
    rows = x.shape[0]
    parts = dot(jnp.concatenate(split3(x), axis=0), exact)
    return parts[:rows] + (parts[rows : 2 * rows] + parts[2 * rows :])


def in_first_half(shape):
    return lax.broadcasted_iota(jnp.int32, shape, len(shape) - 1) < K


def high_low(doubled):
    high = doubled.astype(BF16).astype(F32)
    return jnp.where(in_first_half(doubled.shape), high, doubled - high).astype(BF16)


def add_halves(x):
    return x + pltpu.roll(x, K, axis=1)


def cholesky_rows(a_ref, blocks):
    lanes = a_ref.shape[2]
    for block in blocks:
        first = 4 * block
        start = first // 8 * 8
        rows = tuple(a_ref[first + q, start:K, :] for q in range(4))

        def subtract(k, rows):
            done = a_ref[k, start:K, :]
            return tuple(
                rows[q] - a_ref[k, first + q : first + q + 1, :] * done for q in range(4)
            )

        if first:
            rows = lax.fori_loop(0, first, subtract, rows, unroll=4)
        rows = list(rows)
        index = lax.broadcasted_iota(jnp.int32, (K - start, lanes), 0)
        for q in range(4):
            at = first + q - start
            row = rows[q] * lax.rsqrt(rows[q][at : at + 1, :])
            row = jnp.where(index >= at, row, 0.0)
            a_ref[first + q, start:K, :] = row
            if start:
                a_ref[first + q, 0:start, :] = jnp.zeros((start, lanes), F32)
            for other in range(q + 1, 4):
                into = first + other - start
                rows[other] = rows[other] - row[into : into + 1, :] * row


def tree_gram(basis_ref, inner_ref, x_ref):
    last = inner_ref[:, 14 * PAIR : 15 * PAIR].astype(F32)
    path = [last[:, :K], last[:, K:]]
    for first, count in ((12, 4), (8, 8), (0, 16)):
        longer = []
        for m in range(count // 2):
            both = dot_wide(path[m], inner_ref[:, (first + m) * PAIR : (first + m + 1) * PAIR])
            longer += [both[:, :K], both[:, K:]]
        path = longer
    for m in range(16):
        x = dot_wide(path[m], basis_ref[:, m * PAIR : (m + 1) * PAIR])
        for part, value in enumerate(split3(x)):
            x_ref[part * K : (part + 1) * K, m * PAIR : (m + 1) * PAIR] = value
    parts = dot_nt(x_ref[0:PAIR, :], x_ref[...])
    parts = parts[:K] + parts[K:]
    low = parts[:, PAIR : PAIR + K]
    return (parts[:, :K] + parts[:, K:PAIR] + (low + low.T)) * (1.0 / OWN)


def unpack(ref):
    return jnp.concatenate([ref[:, :K], ref[:, K:]], axis=0)


def kernel_values(exponent):
    return jnp.exp2(exponent * RATIO) + 0.5 * jnp.exp2(exponent)


def leaf_rows(ref, leaf, rows):
    return ref[pl.ds(pl.multiple_of(leaf * rows, rows), rows), :]


def leaf_grams(basis_ref, top, g_ref):
    first = in_first_half((K, PAIR))
    for m in range(OWN // 2):
        v = basis_ref[:, m * PAIR : (m + 1) * PAIR]
        zero = jnp.zeros_like(v)
        one_each = jnp.concatenate([jnp.where(first, v, zero), jnp.where(first, zero, v)], axis=0)
        g_ref[m * PAIR : (m + 1) * PAIR, :] = dot_nt(one_each, v)
    for t in range(OWN, SLOTS):
        g_ref[t * K : (t + 1) * K, :] = top


def to_lanes(g_ref, a_ref):
    count = a_ref.shape[2]
    for i in range(K):
        a_ref[i] = g_ref[pl.ds(i, count, stride=K), :].T


def factor_pairs(a_ref, d_ref, pairs_ref, own_pairs_ref):
    for i in range(K):
        row = a_ref[i]
        d_ref[pl.ds(i, SLOTS, stride=K), :] = jnp.concatenate([row, row], axis=0).T
    first = in_first_half((K, PAIR))
    for t in range(OWN):
        doubled = d_ref[t * K : (t + 1) * K, :]
        high = doubled.astype(BF16).astype(F32)
        low = doubled - high
        pair = jnp.where(first, high, low).astype(BF16)
        pairs_ref[EDGE + t * K : EDGE + (t + 1) * K, :] = pair
        own_pairs_ref[t * PAIR : t * PAIR + K, :] = pair
        own_pairs_ref[t * PAIR + K : (t + 1) * PAIR, :] = jnp.where(first, low, high).astype(BF16)


def place_points(
    first_leaf,
    coords_ref,
    near_ref,
    count_ref,
    source_ref,
    target_ref,
    source_t_ref,
    target_t_ref,
    doubled_ref,
):
    lanes = WIDE * K
    leaf = lax.broadcasted_iota(jnp.int32, (3, lanes), 1) // K
    axis = lax.broadcasted_iota(jnp.int32, (3, lanes), 0)
    corner = jnp.where(
        axis == 0, leaf % 2, jnp.where(axis == 1, leaf // 2 % 2, leaf // LAYER - WIDE // LAYER // 2)
    )
    u = (coords_ref[...] + corner.astype(F32)) * SCALE
    high, middle, low = (part.astype(F32) for part in split3(u))
    norms = [part.astype(F32) for part in split3(-jnp.sum(u * u, axis=0, keepdims=True))]
    ones = jnp.ones((3, lanes), F32)
    own = slice(EDGE, lanes - EDGE)
    for n, (a, b) in enumerate(
        (
            (high, high),
            (high, middle),
            (middle, high),
            (high, low),
            (low, high),
            (middle, middle),
        )
    ):
        target_ref[3 * n : 3 * n + 3, :] = 2.0 * a[:, own]
        source_ref[3 * n : 3 * n + 3, :] = b
    target_ref[18:21, :] = ones[:, own]
    source_ref[21:24, :] = ones
    for n, part in enumerate(norms):
        source_ref[18 + n : 19 + n, :] = part
        target_ref[21 + n : 22 + n, :] = part[:, own]
    source_ref[24:32, :] = jnp.zeros((8, lanes), F32)

    slot = lax.broadcasted_iota(jnp.int32, (NEAR, OWN), 0)
    target = lax.broadcasted_iota(jnp.int32, (NEAR, OWN), 1)
    used = jnp.zeros((NEAR, OWN), jnp.int32)
    for t in range(OWN):
        used = jnp.where(target == t, count_ref[t], used)
    place = near_ref[...] - (first_leaf - LAYER) - target // LAYER * LAYER
    place = jnp.where(slot < used, place, -1)
    window = lax.broadcasted_iota(jnp.int32, (16, OWN), 0)
    bias = jnp.full((16, OWN), OFF, F32)
    for n in range(NEAR):
        bias = jnp.where(place[n : n + 1, :] == window, 0.0, bias)
    spread = lax.broadcasted_iota(jnp.int32, (OWN, OWN * K), 1) // K
    spread = (spread == lax.broadcasted_iota(jnp.int32, (OWN, OWN * K), 0)).astype(F32)
    target_ref[24:40, :] = dot(bias.astype(BF16), spread.astype(BF16))

    target_t_ref[...] = target_ref[...].T.astype(BF16)
    source_t_ref[...] = source_ref[...].T.astype(BF16)
    for t in range(OWN):
        one = target_ref[0:32, t * K : (t + 1) * K]
        doubled_ref[t] = jnp.concatenate([one, one], axis=1).astype(BF16)


def near_layers(layers, source_ref, target_t_ref, vectors_ref, near_out):
    width = LAYER * K
    window = lax.broadcasted_iota(jnp.int32, (16, width), 0)
    column = lax.broadcasted_iota(jnp.int32, (16, width), 1) // K
    for layer in layers:
        total = jnp.zeros((width, vectors_ref.shape[1]), F32)
        for step in range(3):
            at = (layer + 1 + step) * width
            place = (window == column + LAYER * step).astype(F32)
            source = jnp.concatenate([source_ref[0:24, at : at + width], place], axis=0)
            exponent = dot(
                target_t_ref[layer * width : (layer + 1) * width, :], source.astype(BF16)
            )
            weights = kernel_values(exponent).astype(BF16)
            rows = (layer + step) * width
            total = total + dot(weights, vectors_ref[rows : rows + width, :])
        near_out[layer * width : (layer + 1) * width, :] = total.astype(BF16)


def far_leaves(layer, p, at_start, at_end):
    places = []
    for k in range(FAR):
        shift = p - RAD + k + (12 if k + p >= FAR else 0)
        before = max(0, (3 - shift) // 4)
        beyond = max(0, shift // 4)
        place = LAYER * layer + shift
        if before:
            place = place + 15 * at_start * ((7 + before - layer) // 8)
        if beyond:
            place = place - 15 * at_end * ((layer + beyond) // 8)
        places.append(place)
    if isinstance(layer, int):
        places += list(range(11, 15)) if layer == 0 else list(range(17, 21))
    return places


def far_picks(read, names, first_leaf, places):
    values = [read(place + HALO) for place in places]
    picks = []
    for name in names:
        pick = values[0]
        for place, value in zip(places[1:], values[1:]):
            pick = lax.select(name == first_leaf + place, value, pick)
        picks.append(pick)
    return picks


def each_layer(run):
    last = OWN // LAYER - 1
    run(0)

    def step(layer, _):
        run(layer)
        return 0

    lax.fori_loop(1, last, step, 0, unroll=2)
    run(last)


def far_blocks(first_leaf, ends, far_ref, source_t_ref, doubled_ref, block_ref):
    def run(layer):
        for p in range(LAYER):
            t = LAYER * layer + p
            names = [far_ref[f, t] for f in range(FAR)]
            sources = far_picks(
                lambda leaf: leaf_rows(source_t_ref, leaf, K),
                names,
                first_leaf,
                far_leaves(layer, p, *ends),
            )
            exponent = dot(jnp.concatenate(sources, axis=0), doubled_ref[t])
            block_ref[t] = high_low(kernel_values(exponent))

    each_layer(run)


def far_halves(block_ref, own_pairs_ref, half_ref):
    def halves(t, _):
        value = dot_nt(block_ref[t], leaf_rows(own_pairs_ref, t, PAIR))
        half_ref[t] = high_low(add_halves(value) * (1.0 / K))
        return 0

    lax.fori_loop(0, OWN, halves, 0, unroll=4)


def far_products(first_leaf, ends, far_ref, half_ref, pairs_ref, coupling_out):
    def run(layer):
        values = []
        for p in range(LAYER):
            t = LAYER * layer + p
            names = [far_ref[f, t] for f in range(FAR)]
            factors = far_picks(
                lambda leaf: leaf_rows(pairs_ref, leaf, K),
                names,
                first_leaf,
                far_leaves(layer, p, *ends),
            )
            for f in range(FAR):
                half = half_ref[t, f * K : (f + 1) * K, :]
                values.append(add_halves(dot(factors[f], jnp.concatenate([half, half], axis=0))))
        first = in_first_half((K, PAIR))
        both = [jnp.where(first, values[2 * n], values[2 * n + 1]) for n in range(2 * FAR)]
        at = pl.multiple_of(layer * 2 * FAR * PAIR, PAIR)
        coupling_out[:, pl.ds(at, 2 * FAR * PAIR)] = jnp.concatenate(both, axis=1).astype(BF16)

    each_layer(run)


def turned(index, stride, size, by):
    at = lax.rem(index // stride, size)
    return index + (lax.rem(at + by, size) - at) * stride


def upsweep_kernel(
    count_ref,
    far_ref,
    basis_hbm,
    inner_hbm,
    transfer_hbm,
    points_hbm,
    near_hbm,
    vectors_hbm,
    near_hbm_out,
    coupling_hbm_out,
    factor_out,
    group_sum_out,
    root_sum_out,
    near_out,
    coupling_out,
    basis_ref,
    inner_ref,
    transfer_ref,
    near_ref,
    coords_ref,
    vectors_ref,
    g_ref,
    d_ref,
    a_ref,
    x_ref,
    pairs_ref,
    own_pairs_ref,
    source_ref,
    target_ref,
    source_t_ref,
    target_t_ref,
    doubled_ref,
    block_ref,
    half_ref,
    sum_ref,
    got_ref,
    in_sem,
    out_sem,
    send_sem,
    recv_sem,
):
    groups, subs = lax.axis_size("group"), lax.axis_size("sub")
    g, s = lax.axis_index("group"), lax.axis_index("sub")
    me = g * subs + s
    first_leaf = me * OWN
    count = groups * subs
    ends = ((count - me) // count, (me + 1) // count)
    after = lax.rem(me + 1, groups * subs)
    before = lax.rem(me + groups * subs - 1, groups * subs)
    after = (after // subs, lax.rem(after, subs))
    before = (before // subs, lax.rem(before, subs))

    plane = [
        (g, turned(turned(s, 2, 4, x), 8, 4, y)) for x in range(4) for y in range(4) if x or y
    ]
    steps = [(core, z) for core in range(2) for z in (0, 1, 2, 15) if core or z]
    window = [(turned(g, 1, 16, 16 - z), turned(s, 1, 2, core)) for core, z in steps]
    senders = [(turned(g, 1, 16, z), turned(s, 1, 2, core)) for core, z in steps]
    cover = [(turned(g, 1, 16, z), s) for z in (2, 6, 10, 14)]

    barrier = pltpu.get_barrier_semaphore()
    greeted = cover + senders + plane + [after, before]
    for device in greeted:
        pl.semaphore_signal(barrier, inc=1, device_id=device, device_id_type=MESH)

    lanes, rows = points_hbm.shape[1], vectors_hbm.shape[0]
    loads = [
        pltpu.make_async_copy(source, target, in_sem.at[n])
        for n, (source, target) in enumerate(
            (
                (inner_hbm, inner_ref),
                (basis_hbm, basis_ref),
                (transfer_hbm, transfer_ref),
                (points_hbm, coords_ref.at[:, EDGE : EDGE + lanes]),
                (near_hbm, near_ref),
                (vectors_hbm, vectors_ref.at[LAYER * K : LAYER * K + rows]),
            )
        )
    ]
    for load in loads:
        load.start()
    for load in loads[:3]:
        load.wait()

    top = tree_gram(basis_ref, inner_ref, x_ref)
    transfer = transfer_ref[...]
    gram = exact_dot_t(transfer, exact_dot(top, transfer))
    sum_ref[0] = jnp.concatenate([gram[: K // 2], gram[K // 2 :]], axis=1)

    leaf_grams(basis_ref, top, g_ref)
    to_lanes(g_ref, a_ref)
    cholesky_rows(a_ref, range(0, FIRST_PART))

    pl.semaphore_wait(barrier, len(greeted))

    def copy(number, source, target, device):
        return pltpu.make_async_remote_copy(
            src_ref=source,
            dst_ref=target,
            send_sem=send_sem.at[number],
            recv_sem=recv_sem.at[number],
            device_id=device,
            device_id_type=MESH,
        )

    def send(stage, first, devices):
        copies = [
            copy(first + n, sum_ref.at[stage], got_ref.at[first + n], device)
            for n, device in enumerate(devices)
        ]
        for one in copies:
            one.start()
        return copies

    def gather(total, first, copies):
        for n, one in enumerate(copies):
            one.wait()
            total = total + got_ref[first + n]
        return total

    sent = send(0, 0, plane)
    for load in loads[3:]:
        load.wait()
    halos = [
        copy(SUMS, coords_ref.at[:, lanes : lanes + EDGE], coords_ref.at[:, 0:EDGE], after),
        copy(
            SUMS + 1,
            coords_ref.at[:, EDGE : 2 * EDGE],
            coords_ref.at[:, EDGE + lanes : 2 * EDGE + lanes],
            before,
        ),
        copy(
            SUMS + 2,
            vectors_ref.at[rows : rows + LAYER * K],
            vectors_ref.at[0 : LAYER * K],
            after,
        ),
        copy(
            SUMS + 3,
            vectors_ref.at[LAYER * K : 2 * LAYER * K],
            vectors_ref.at[rows + LAYER * K : rows + 2 * LAYER * K],
            before,
        ),
    ]
    for halo in halos:
        halo.start()

    cholesky_rows(a_ref, range(FIRST_PART, 16))
    factor_pairs(a_ref, d_ref, pairs_ref, own_pairs_ref)
    edges = [
        copy(SUMS + 4, pairs_ref.at[OWN * K : OWN * K + EDGE], pairs_ref.at[0:EDGE], after),
        copy(
            SUMS + 5,
            pairs_ref.at[EDGE : 2 * EDGE],
            pairs_ref.at[OWN * K + EDGE : OWN * K + 2 * EDGE],
            before,
        ),
    ]
    for edge in edges:
        edge.start()
    factor_out[...] = exact_dot(d_ref[OWN * K : (OWN + 1) * K, 0:K], transfer)

    sum_ref[1] = gather(sum_ref[0], 0, sent)
    sent = send(1, PLANE, window)
    for halo in halos:
        halo.wait()
    place_points(
        first_leaf,
        coords_ref,
        near_ref,
        count_ref,
        source_ref,
        target_ref,
        source_t_ref,
        target_t_ref,
        doubled_ref,
    )
    far_blocks(first_leaf, ends, far_ref, source_t_ref, doubled_ref, block_ref)
    sum_ref[2] = gather(sum_ref[1], PLANE, sent)
    group_sum_out[...] = sum_ref[1] + got_ref[PLANE + steps.index((1, 0))]
    sent = send(2, PLANE + WINDOW, cover)
    near_layers(range(OWN // LAYER), source_ref, target_t_ref, vectors_ref, near_out)
    near_move = pltpu.make_async_copy(near_out, near_hbm_out, out_sem.at[0])
    near_move.start()
    far_halves(block_ref, own_pairs_ref, half_ref)
    for edge in edges:
        edge.wait()
    far_products(first_leaf, ends, far_ref, half_ref, pairs_ref, coupling_out)
    coupling_move = pltpu.make_async_copy(coupling_out, coupling_hbm_out, out_sem.at[1])
    coupling_move.start()
    root_sum_out[...] = gather(jnp.zeros((K // 2, PAIR), F32), PLANE + WINDOW, sent)
    near_move.wait()
    coupling_move.wait()


def upsweep_call(near_count, far_t, basis_t, inner_t, transfer, points, near_t, vectors):
    whole = pl.BlockSpec(memory_space=pltpu.VMEM)
    scalars = pl.BlockSpec(memory_space=pltpu.SMEM)
    anywhere = pl.BlockSpec(memory_space=pltpu.HBM)
    packed = jax.ShapeDtypeStruct((K // 2, PAIR), F32)
    rows, columns = vectors.shape
    return pl.pallas_call(
        upsweep_kernel,
        out_shape=(
            jax.ShapeDtypeStruct(vectors.shape, BF16),
            jax.ShapeDtypeStruct((K, FAR * OWN * K), BF16),
            jax.ShapeDtypeStruct((K, K), F32),
            packed,
            packed,
        ),
        in_specs=[scalars] * 2 + [anywhere] * INPUTS,
        out_specs=(anywhere,) * 2 + (whole,) * 3,
        scratch_shapes=[
            pltpu.VMEM(vectors.shape, BF16),
            pltpu.VMEM((K, FAR * OWN * K), BF16),
            pltpu.VMEM(basis_t.shape, BF16),
            pltpu.VMEM(inner_t.shape, BF16),
            pltpu.VMEM((K, K), F32),
            pltpu.VMEM(near_t.shape, jnp.int32),
            pltpu.VMEM((3, WIDE * K), F32),
            pltpu.VMEM((rows + 2 * LAYER * K, columns), BF16),
            pltpu.VMEM((SLOTS * K, K), F32),
            pltpu.VMEM((SLOTS * K, PAIR), F32),
            pltpu.VMEM((K, K, SLOTS), F32),
            pltpu.VMEM((3 * K, OWN * K), BF16),
            pltpu.VMEM((WIDE * K, PAIR), BF16),
            pltpu.VMEM((OWN * PAIR, PAIR), BF16),
            pltpu.VMEM((32, WIDE * K), F32),
            pltpu.VMEM((40, OWN * K), F32),
            pltpu.VMEM((WIDE * K, 32), BF16),
            pltpu.VMEM((OWN * K, 40), BF16),
            pltpu.VMEM((OWN, 32, PAIR), BF16),
            pltpu.VMEM((OWN, FAR * K, PAIR), BF16),
            pltpu.VMEM((OWN, FAR * K, PAIR), BF16),
            pltpu.VMEM((3, K // 2, PAIR), F32),
            pltpu.VMEM((SUMS, K // 2, PAIR), F32),
            pltpu.SemaphoreType.DMA((INPUTS,)),
            pltpu.SemaphoreType.DMA((2,)),
            pltpu.SemaphoreType.DMA((COPIES,)),
            pltpu.SemaphoreType.DMA((COPIES,)),
        ],
        compiler_params=pltpu.CompilerParams(
            collective_id=0, has_side_effects=True, vmem_limit_bytes=VMEM_LIMIT
        ),
    )(near_count, far_t, basis_t, inner_t, transfer, points, near_t, vectors)


def unpack(ref):
    return jnp.concatenate([ref[:, :K], ref[:, K:]], axis=0)


def last_kernel(
    group_sum,
    root_sum,
    factor_ref,
    near_ref,
    coupling_ref,
    near_out,
    coupling_out,
    factor_out,
    group_out,
    root_out,
    g_ref,
    a_ref,
    sem,
):
    moves = [
        pltpu.make_async_copy(near_ref, near_out, sem.at[0]),
        pltpu.make_async_copy(coupling_ref, coupling_out, sem.at[1]),
    ]
    for move in moves:
        move.start()
    groups, subs = lax.axis_size("group"), lax.axis_size("sub")
    factor_out[...] = factor_ref[...]
    group = unpack(group_sum[...]) * (1.0 / subs)
    root = unpack(root_sum[...]) * (1.0 / (subs * groups))
    for n in range(8):
        g_ref[n * K : (n + 1) * K, :] = root if n else group
    to_lanes(g_ref, a_ref)
    cholesky_rows(a_ref, range(16))
    for i in range(K):
        g_ref[pl.ds(i, 8, stride=K), :] = a_ref[i].T
    group_out[...] = g_ref[0:K, :]
    root_out[...] = g_ref[K : 2 * K, :]
    for move in moves:
        move.wait()


def last_call(group_sum, root_sum, factor, near, coupling_t):
    whole = pl.BlockSpec(memory_space=pltpu.VMEM)
    anywhere = pl.BlockSpec(memory_space=pl.ANY)
    square = jax.ShapeDtypeStruct((K, K), F32)
    return pl.pallas_call(
        last_kernel,
        out_shape=(
            jax.ShapeDtypeStruct(near.shape, BF16),
            jax.ShapeDtypeStruct(coupling_t.shape, BF16),
            square,
            square,
            square,
        ),
        in_specs=[whole] * 3 + [anywhere] * 2,
        out_specs=(anywhere,) * 2 + (whole,) * 3,
        scratch_shapes=[
            pltpu.VMEM((8 * K, K), F32),
            pltpu.VMEM((K, K, 8), F32),
            pltpu.SemaphoreType.DMA((2,)),
        ],
        compiler_params=pltpu.CompilerParams(vmem_limit_bytes=VMEM_LIMIT),
    )(group_sum, root_sum, factor, near, coupling_t)


def per_device(
    points, leaf_basis, inner_transfer, device_transfer, vectors, near_index, near_count, far_index
):
    near, coupling_t, factor, group_sum, root_sum = upsweep_call(
        near_count,
        far_index.T,
        leaf_basis.T,
        inner_transfer.T,
        device_transfer,
        points,
        near_index.T,
        vectors,
    )
    near_product, coupling_t, device_factor, group_factor, root_factor = last_call(
        group_sum, root_sum, factor, near, coupling_t
    )
    return near_product, coupling_t.T, device_factor, group_factor, root_factor


def solution(mesh):
    rows = P(("group", "sub"), None)
    return jax.shard_map(
        per_device,
        mesh=mesh,
        in_specs=(
            P(None, ("group", "sub")),
            rows,
            rows,
            rows,
            rows,
            rows,
            P(("group", "sub")),
            rows,
        ),
        out_specs=(rows,) * 5,
        check_vma=False,
    )
```

```python
import math

import jax
import jax.numpy as jnp
from jax import lax
from jax.experimental import pallas as pl
from jax.experimental.pallas import tpu as pltpu
from jax.sharding import PartitionSpec as P

K = 64
PAIR = 2 * K
LAYER = 4
RAD = 7
NEAR = 12
FAR = 3
HALO = 8
OWN = 32
WIDE = OWN + 2 * HALO
EDGE = HALO * K
SLOTS = 40
SHORT_SQ = 0.09
LONG_SQ = 2.25
RATIO = LONG_SQ / SHORT_SQ
SCALE = math.sqrt(0.5 / LONG_SQ * math.log2(math.e))
OFF = -131072.0
VMEM_LIMIT = 60 << 20
F32 = jnp.float32
BF16 = jnp.bfloat16
MESH = pl.DeviceIdType.MESH
PLANE = 15
WINDOW = 7
COVER = 4
SUMS = PLANE + WINDOW + COVER
COPIES = SUMS + 6
INPUTS = 6
FIRST_PART = 10


def dot(a, b):
    return jnp.dot(a, b, preferred_element_type=F32)


def dot_nt(a, b):
    return lax.dot_general(a, b, (((1,), (1,)), ((), ())), preferred_element_type=F32)


def exact_dot(a, b):
    return jnp.dot(a, b, preferred_element_type=F32, precision=lax.Precision.HIGHEST)


def exact_dot_t(a, b):
    return lax.dot_general(
        a, b, (((0,), (0,)), ((), ())), preferred_element_type=F32, precision=lax.Precision.HIGHEST
    )


def split3(x):
    high = x.astype(BF16)
    rest = x - high.astype(F32)
    middle = rest.astype(BF16)
    low = (rest - middle.astype(F32)).astype(BF16)
    return high, middle, low


def dot_wide(x, exact):
    rows = x.shape[0]
    parts = dot(jnp.concatenate(split3(x), axis=0), exact)
    return parts[:rows] + (parts[rows : 2 * rows] + parts[2 * rows :])


def in_first_half(shape):
    return lax.broadcasted_iota(jnp.int32, shape, len(shape) - 1) < K


def high_low(doubled):
    high = doubled.astype(BF16).astype(F32)
    return jnp.where(in_first_half(doubled.shape), high, doubled - high).astype(BF16)


def add_halves(x):
    return x + pltpu.roll(x, K, axis=1)


def cholesky_rows(a_ref, blocks, unroll=4):
    lanes = a_ref.shape[2]
    for block in blocks:
        first = 4 * block
        start = first // 8 * 8
        rows = tuple(a_ref[first + q, start:K, :] for q in range(4))

        def subtract(k, rows):
            done = a_ref[k, start:K, :]
            return tuple(
                rows[q] - a_ref[k, first + q : first + q + 1, :] * done for q in range(4)
            )

        if first:
            rows = lax.fori_loop(0, first, subtract, rows, unroll=unroll)
        rows = list(rows)
        index = lax.broadcasted_iota(jnp.int32, (K - start, lanes), 0)
        for q in range(4):
            at = first + q - start
            row = rows[q] * lax.rsqrt(rows[q][at : at + 1, :])
            row = jnp.where(index >= at, row, 0.0)
            a_ref[first + q, start:K, :] = row
            if start:
                a_ref[first + q, 0:start, :] = jnp.zeros((start, lanes), F32)
            for other in range(q + 1, 4):
                into = first + other - start
                rows[other] = rows[other] - row[into : into + 1, :] * row


def tree_gram(basis_ref, inner_ref, x_ref):
    last = inner_ref[:, 14 * PAIR : 15 * PAIR].astype(F32)
    path = [last[:, :K], last[:, K:]]
    for first, count in ((12, 4), (8, 8), (0, 16)):
        longer = []
        for m in range(count // 2):
            both = dot_wide(path[m], inner_ref[:, (first + m) * PAIR : (first + m + 1) * PAIR])
            longer += [both[:, :K], both[:, K:]]
        path = longer
    for m in range(16):
        x = dot_wide(path[m], basis_ref[:, m * PAIR : (m + 1) * PAIR])
        for part, value in enumerate(split3(x)):
            x_ref[part * K : (part + 1) * K, m * PAIR : (m + 1) * PAIR] = value
    parts = dot_nt(x_ref[0:PAIR, :], x_ref[...])
    parts = parts[:K] + parts[K:]
    low = parts[:, PAIR : PAIR + K]
    return (parts[:, :K] + parts[:, K:PAIR] + (low + low.T)) * (1.0 / OWN)


def unpack(ref):
    return jnp.concatenate([ref[:, :K], ref[:, K:]], axis=0)


def kernel_values(exponent):
    return jnp.exp2(exponent * RATIO) + 0.5 * jnp.exp2(exponent)


def leaf_rows(ref, leaf, rows):
    return ref[pl.ds(pl.multiple_of(leaf * rows, rows), rows), :]


def leaf_grams(basis_ref, top, g_ref):
    first = in_first_half((K, PAIR))
    for m in range(OWN // 2):
        v = basis_ref[:, m * PAIR : (m + 1) * PAIR]
        zero = jnp.zeros_like(v)
        one_each = jnp.concatenate([jnp.where(first, v, zero), jnp.where(first, zero, v)], axis=0)
        g_ref[m * PAIR : (m + 1) * PAIR, :] = dot_nt(one_each, v)
    for t in range(OWN, SLOTS):
        g_ref[t * K : (t + 1) * K, :] = top


def to_lanes(g_ref, a_ref):
    count = a_ref.shape[2]
    for i in range(K):
        a_ref[i] = g_ref[pl.ds(i, count, stride=K), :].T


def factor_pairs(a_ref, d_ref, pairs_ref, own_pairs_ref):
    for i in range(K):
        row = a_ref[i]
        d_ref[pl.ds(i, SLOTS, stride=K), :] = jnp.concatenate([row, row], axis=0).T
    first = in_first_half((K, PAIR))
    for t in range(OWN):
        doubled = d_ref[t * K : (t + 1) * K, :]
        high = doubled.astype(BF16).astype(F32)
        low = doubled - high
        pair = jnp.where(first, high, low).astype(BF16)
        pairs_ref[EDGE + t * K : EDGE + (t + 1) * K, :] = pair
        own_pairs_ref[t * PAIR : t * PAIR + K, :] = pair
        own_pairs_ref[t * PAIR + K : (t + 1) * PAIR, :] = jnp.where(first, low, high).astype(BF16)


def place_points(
    first_leaf,
    coords_ref,
    near_ref,
    count_ref,
    source_ref,
    target_ref,
    source_t_ref,
    target_t_ref,
    doubled_ref,
):
    lanes = WIDE * K
    leaf = lax.broadcasted_iota(jnp.int32, (3, lanes), 1) // K
    axis = lax.broadcasted_iota(jnp.int32, (3, lanes), 0)
    corner = jnp.where(
        axis == 0, leaf % 2, jnp.where(axis == 1, leaf // 2 % 2, leaf // LAYER - WIDE // LAYER // 2)
    )
    u = (coords_ref[...] + corner.astype(F32)) * SCALE
    high, middle, low = (part.astype(F32) for part in split3(u))
    norms = [part.astype(F32) for part in split3(-jnp.sum(u * u, axis=0, keepdims=True))]
    ones = jnp.ones((3, lanes), F32)
    own = slice(EDGE, lanes - EDGE)
    for n, (a, b) in enumerate(
        (
            (high, high),
            (high, middle),
            (middle, high),
            (high, low),
            (low, high),
            (middle, middle),
        )
    ):
        target_ref[3 * n : 3 * n + 3, :] = 2.0 * a[:, own]
        source_ref[3 * n : 3 * n + 3, :] = b
    target_ref[18:21, :] = ones[:, own]
    source_ref[21:24, :] = ones
    for n, part in enumerate(norms):
        source_ref[18 + n : 19 + n, :] = part
        target_ref[21 + n : 22 + n, :] = part[:, own]
    source_ref[24:32, :] = jnp.zeros((8, lanes), F32)

    slot = lax.broadcasted_iota(jnp.int32, (NEAR, OWN), 0)
    target = lax.broadcasted_iota(jnp.int32, (NEAR, OWN), 1)
    used = jnp.zeros((NEAR, OWN), jnp.int32)
    for t in range(OWN):
        used = jnp.where(target == t, count_ref[t], used)
    place = near_ref[...] - (first_leaf - LAYER) - target // LAYER * LAYER
    place = jnp.where(slot < used, place, -1)
    window = lax.broadcasted_iota(jnp.int32, (16, OWN), 0)
    bias = jnp.full((16, OWN), OFF, F32)
    for n in range(NEAR):
        bias = jnp.where(place[n : n + 1, :] == window, 0.0, bias)
    spread = lax.broadcasted_iota(jnp.int32, (OWN, OWN * K), 1) // K
    spread = (spread == lax.broadcasted_iota(jnp.int32, (OWN, OWN * K), 0)).astype(F32)
    target_ref[24:40, :] = dot(bias.astype(BF16), spread.astype(BF16))

    target_t_ref[...] = target_ref[...].T.astype(BF16)
    source_t_ref[...] = source_ref[...].T.astype(BF16)
    for t in range(OWN):
        one = target_ref[0:32, t * K : (t + 1) * K]
        doubled_ref[t] = jnp.concatenate([one, one], axis=1).astype(BF16)


def near_layers(layers, source_ref, target_t_ref, vectors_ref, near_out):
    width = LAYER * K
    window = lax.broadcasted_iota(jnp.int32, (16, width), 0)
    column = lax.broadcasted_iota(jnp.int32, (16, width), 1) // K
    for layer in layers:
        total = jnp.zeros((width, vectors_ref.shape[1]), F32)
        for step in range(3):
            at = (layer + 1 + step) * width
            place = (window == column + LAYER * step).astype(F32)
            source = jnp.concatenate([source_ref[0:24, at : at + width], place], axis=0)
            exponent = dot(
                target_t_ref[layer * width : (layer + 1) * width, :], source.astype(BF16)
            )
            weights = kernel_values(exponent).astype(BF16)
            rows = (layer + step) * width
            total = total + dot(weights, vectors_ref[rows : rows + width, :])
        near_out[layer * width : (layer + 1) * width, :] = total.astype(BF16)


def far_leaves(layer, p, at_start, at_end):
    places = []
    for k in range(FAR):
        shift = p - RAD + k + (12 if k + p >= FAR else 0)
        before = max(0, (3 - shift) // 4)
        beyond = max(0, shift // 4)
        place = LAYER * layer + shift
        if before:
            place = place + 15 * at_start * ((7 + before - layer) // 8)
        if beyond:
            place = place - 15 * at_end * ((layer + beyond) // 8)
        places.append(place)
    if isinstance(layer, int):
        places += list(range(11, 15)) if layer == 0 else list(range(17, 21))
    return places


def far_picks(read, names, first_leaf, places):
    values = [read(place + HALO) for place in places]
    picks = []
    for name in names:
        pick = values[0]
        for place, value in zip(places[1:], values[1:]):
            pick = lax.select(name == first_leaf + place, value, pick)
        picks.append(pick)
    return picks


def each_layer(run):
    last = OWN // LAYER - 1
    run(0)

    def step(layer, _):
        run(layer)
        return 0

    lax.fori_loop(1, last, step, 0, unroll=2)
    run(last)


def far_blocks(first_leaf, ends, far_ref, source_t_ref, doubled_ref, block_ref):
    def run(layer):
        for p in range(LAYER):
            t = LAYER * layer + p
            names = [far_ref[f, t] for f in range(FAR)]
            sources = far_picks(
                lambda leaf: leaf_rows(source_t_ref, leaf, K),
                names,
                first_leaf,
                far_leaves(layer, p, *ends),
            )
            exponent = dot(jnp.concatenate(sources, axis=0), doubled_ref[t])
            block_ref[t] = high_low(kernel_values(exponent))

    each_layer(run)


def far_halves(block_ref, own_pairs_ref, half_ref):
    def halves(t, _):
        value = dot_nt(block_ref[t], leaf_rows(own_pairs_ref, t, PAIR))
        half_ref[t] = high_low(add_halves(value) * (1.0 / K))
        return 0

    lax.fori_loop(0, OWN, halves, 0, unroll=4)


def far_products(first_leaf, ends, far_ref, half_ref, pairs_ref, coupling_out):
    def run(layer):
        values = []
        for p in range(LAYER):
            t = LAYER * layer + p
            names = [far_ref[f, t] for f in range(FAR)]
            factors = far_picks(
                lambda leaf: leaf_rows(pairs_ref, leaf, K),
                names,
                first_leaf,
                far_leaves(layer, p, *ends),
            )
            for f in range(FAR):
                half = half_ref[t, f * K : (f + 1) * K, :]
                values.append(add_halves(dot(factors[f], jnp.concatenate([half, half], axis=0))))
        first = in_first_half((K, PAIR))
        both = [jnp.where(first, values[2 * n], values[2 * n + 1]) for n in range(2 * FAR)]
        at = pl.multiple_of(layer * 2 * FAR * PAIR, PAIR)
        coupling_out[:, pl.ds(at, 2 * FAR * PAIR)] = jnp.concatenate(both, axis=1).astype(BF16)

    each_layer(run)


def turned(index, stride, size, by):
    at = lax.rem(index // stride, size)
    return index + (lax.rem(at + by, size) - at) * stride


def upsweep_kernel(
    count_ref,
    far_ref,
    basis_hbm,
    inner_hbm,
    transfer_hbm,
    points_hbm,
    near_hbm,
    vectors_hbm,
    near_hbm_out,
    coupling_hbm_out,
    factor_out,
    group_sum_out,
    root_sum_out,
    near_out,
    coupling_out,
    basis_ref,
    inner_ref,
    transfer_ref,
    near_ref,
    coords_ref,
    vectors_ref,
    g_ref,
    d_ref,
    a_ref,
    x_ref,
    pairs_ref,
    own_pairs_ref,
    source_ref,
    target_ref,
    source_t_ref,
    target_t_ref,
    doubled_ref,
    block_ref,
    half_ref,
    sum_ref,
    got_ref,
    in_sem,
    out_sem,
    send_sem,
    recv_sem,
):
    groups, subs = lax.axis_size("group"), lax.axis_size("sub")
    g, s = lax.axis_index("group"), lax.axis_index("sub")
    me = g * subs + s
    first_leaf = me * OWN
    count = groups * subs
    ends = ((count - me) // count, (me + 1) // count)
    after = lax.rem(me + 1, groups * subs)
    before = lax.rem(me + groups * subs - 1, groups * subs)
    after = (after // subs, lax.rem(after, subs))
    before = (before // subs, lax.rem(before, subs))

    plane = [
        (g, turned(turned(s, 2, 4, x), 8, 4, y)) for x in range(4) for y in range(4) if x or y
    ]
    steps = [(core, z) for core in range(2) for z in (0, 1, 2, 15) if core or z]
    window = [(turned(g, 1, 16, 16 - z), turned(s, 1, 2, core)) for core, z in steps]
    senders = [(turned(g, 1, 16, z), turned(s, 1, 2, core)) for core, z in steps]
    cover = [(turned(g, 1, 16, z), s) for z in (2, 6, 10, 14)]

    barrier = pltpu.get_barrier_semaphore()
    greeted = cover + senders + plane + [after, before]
    for device in greeted:
        pl.semaphore_signal(barrier, inc=1, device_id=device, device_id_type=MESH)

    lanes, rows = points_hbm.shape[1], vectors_hbm.shape[0]
    loads = [
        pltpu.make_async_copy(source, target, in_sem.at[n])
        for n, (source, target) in enumerate(
            (
                (inner_hbm, inner_ref),
                (basis_hbm, basis_ref),
                (transfer_hbm, transfer_ref),
                (points_hbm, coords_ref.at[:, EDGE : EDGE + lanes]),
                (near_hbm, near_ref),
                (vectors_hbm, vectors_ref.at[LAYER * K : LAYER * K + rows]),
            )
        )
    ]
    for load in loads:
        load.start()
    for load in loads[:3]:
        load.wait()

    top = tree_gram(basis_ref, inner_ref, x_ref)
    transfer = transfer_ref[...]
    gram = exact_dot_t(transfer, exact_dot(top, transfer))
    sum_ref[0] = jnp.concatenate([gram[: K // 2], gram[K // 2 :]], axis=1)

    leaf_grams(basis_ref, top, g_ref)
    to_lanes(g_ref, a_ref)
    cholesky_rows(a_ref, range(0, FIRST_PART))

    pl.semaphore_wait(barrier, len(greeted))

    def copy(number, source, target, device):
        return pltpu.make_async_remote_copy(
            src_ref=source,
            dst_ref=target,
            send_sem=send_sem.at[number],
            recv_sem=recv_sem.at[number],
            device_id=device,
            device_id_type=MESH,
        )

    def send(stage, first, devices):
        copies = [
            copy(first + n, sum_ref.at[stage], got_ref.at[first + n], device)
            for n, device in enumerate(devices)
        ]
        for one in copies:
            one.start()
        return copies

    def gather(total, first, copies):
        for n, one in enumerate(copies):
            one.wait()
            total = total + got_ref[first + n]
        return total

    sent = send(0, 0, plane)
    for load in loads[3:]:
        load.wait()
    halos = [
        copy(SUMS, coords_ref.at[:, lanes : lanes + EDGE], coords_ref.at[:, 0:EDGE], after),
        copy(
            SUMS + 1,
            coords_ref.at[:, EDGE : 2 * EDGE],
            coords_ref.at[:, EDGE + lanes : 2 * EDGE + lanes],
            before,
        ),
        copy(
            SUMS + 2,
            vectors_ref.at[rows : rows + LAYER * K],
            vectors_ref.at[0 : LAYER * K],
            after,
        ),
        copy(
            SUMS + 3,
            vectors_ref.at[LAYER * K : 2 * LAYER * K],
            vectors_ref.at[rows + LAYER * K : rows + 2 * LAYER * K],
            before,
        ),
    ]
    for halo in halos:
        halo.start()

    cholesky_rows(a_ref, range(FIRST_PART, 16))
    factor_pairs(a_ref, d_ref, pairs_ref, own_pairs_ref)
    edges = [
        copy(SUMS + 4, pairs_ref.at[OWN * K : OWN * K + EDGE], pairs_ref.at[0:EDGE], after),
        copy(
            SUMS + 5,
            pairs_ref.at[EDGE : 2 * EDGE],
            pairs_ref.at[OWN * K + EDGE : OWN * K + 2 * EDGE],
            before,
        ),
    ]
    for edge in edges:
        edge.start()
    factor_out[...] = exact_dot(d_ref[OWN * K : (OWN + 1) * K, 0:K], transfer)

    for halo in halos[:2]:
        halo.wait()
    place_points(
        first_leaf,
        coords_ref,
        near_ref,
        count_ref,
        source_ref,
        target_ref,
        source_t_ref,
        target_t_ref,
        doubled_ref,
    )
    near_layers(range(1, 5), source_ref, target_t_ref, vectors_ref, near_out)
    sum_ref[1] = gather(sum_ref[0], 0, sent)
    sent = send(1, PLANE, window)
    far_blocks(first_leaf, ends, far_ref, source_t_ref, doubled_ref, block_ref)
    near_layers(range(5, 7), source_ref, target_t_ref, vectors_ref, near_out)
    sum_ref[2] = gather(sum_ref[1], PLANE, sent)
    group_sum_out[...] = sum_ref[1] + got_ref[PLANE + steps.index((1, 0))]
    sent = send(2, PLANE + WINDOW, cover)
    for halo in halos[2:]:
        halo.wait()
    near_layers((0, 7), source_ref, target_t_ref, vectors_ref, near_out)
    near_move = pltpu.make_async_copy(near_out, near_hbm_out, out_sem.at[0])
    near_move.start()
    far_halves(block_ref, own_pairs_ref, half_ref)
    for edge in edges:
        edge.wait()
    far_products(first_leaf, ends, far_ref, half_ref, pairs_ref, coupling_out)
    coupling_move = pltpu.make_async_copy(coupling_out, coupling_hbm_out, out_sem.at[1])
    coupling_move.start()
    root_sum_out[...] = gather(jnp.zeros((K // 2, PAIR), F32), PLANE + WINDOW, sent)
    near_move.wait()
    coupling_move.wait()


def upsweep_call(near_count, far_t, basis_t, inner_t, transfer, points, near_t, vectors):
    whole = pl.BlockSpec(memory_space=pltpu.VMEM)
    scalars = pl.BlockSpec(memory_space=pltpu.SMEM)
    anywhere = pl.BlockSpec(memory_space=pltpu.HBM)
    packed = jax.ShapeDtypeStruct((K // 2, PAIR), F32)
    rows, columns = vectors.shape
    return pl.pallas_call(
        upsweep_kernel,
        out_shape=(
            jax.ShapeDtypeStruct(vectors.shape, BF16),
            jax.ShapeDtypeStruct((K, FAR * OWN * K), BF16),
            jax.ShapeDtypeStruct((K, K), F32),
            packed,
            packed,
        ),
        in_specs=[scalars] * 2 + [anywhere] * INPUTS,
        out_specs=(anywhere,) * 2 + (whole,) * 3,
        scratch_shapes=[
            pltpu.VMEM(vectors.shape, BF16),
            pltpu.VMEM((K, FAR * OWN * K), BF16),
            pltpu.VMEM(basis_t.shape, BF16),
            pltpu.VMEM(inner_t.shape, BF16),
            pltpu.VMEM((K, K), F32),
            pltpu.VMEM(near_t.shape, jnp.int32),
            pltpu.VMEM((3, WIDE * K), F32),
            pltpu.VMEM((rows + 2 * LAYER * K, columns), BF16),
            pltpu.VMEM((SLOTS * K, K), F32),
            pltpu.VMEM((SLOTS * K, PAIR), F32),
            pltpu.VMEM((K, K, SLOTS), F32),
            pltpu.VMEM((3 * K, OWN * K), BF16),
            pltpu.VMEM((WIDE * K, PAIR), BF16),
            pltpu.VMEM((OWN * PAIR, PAIR), BF16),
            pltpu.VMEM((32, WIDE * K), F32),
            pltpu.VMEM((40, OWN * K), F32),
            pltpu.VMEM((WIDE * K, 32), BF16),
            pltpu.VMEM((OWN * K, 40), BF16),
            pltpu.VMEM((OWN, 32, PAIR), BF16),
            pltpu.VMEM((OWN, FAR * K, PAIR), BF16),
            pltpu.VMEM((OWN, FAR * K, PAIR), BF16),
            pltpu.VMEM((3, K // 2, PAIR), F32),
            pltpu.VMEM((SUMS, K // 2, PAIR), F32),
            pltpu.SemaphoreType.DMA((INPUTS,)),
            pltpu.SemaphoreType.DMA((2,)),
            pltpu.SemaphoreType.DMA((COPIES,)),
            pltpu.SemaphoreType.DMA((COPIES,)),
        ],
        compiler_params=pltpu.CompilerParams(
            collective_id=0, has_side_effects=True, vmem_limit_bytes=VMEM_LIMIT
        ),
    )(near_count, far_t, basis_t, inner_t, transfer, points, near_t, vectors)


def unpack(ref):
    return jnp.concatenate([ref[:, :K], ref[:, K:]], axis=0)


def last_kernel(
    group_sum,
    root_sum,
    factor_ref,
    near_ref,
    coupling_ref,
    near_out,
    coupling_out,
    factor_out,
    group_out,
    root_out,
    near_buffer,
    coupling_buffer,
    g_ref,
    a_ref,
    sem,
):
    arrivals = [
        pltpu.make_async_copy(near_ref, near_buffer, sem.at[0]),
        pltpu.make_async_copy(coupling_ref, coupling_buffer, sem.at[1]),
    ]
    departures = [
        pltpu.make_async_copy(near_buffer, near_out, sem.at[2]),
        pltpu.make_async_copy(coupling_buffer, coupling_out, sem.at[3]),
    ]
    for arrival in arrivals:
        arrival.start()
    groups, subs = lax.axis_size("group"), lax.axis_size("sub")
    factor_out[...] = factor_ref[...]
    group = unpack(group_sum[...]) * (1.0 / subs)
    root = unpack(root_sum[...]) * (1.0 / (subs * groups))
    for n in range(8):
        g_ref[n * K : (n + 1) * K, :] = root if n else group
    to_lanes(g_ref, a_ref)
    cholesky_rows(a_ref, range(8), unroll=True)
    for arrival, departure in zip(arrivals, departures):
        arrival.wait()
        departure.start()
    cholesky_rows(a_ref, range(8, 16), unroll=True)
    for i in range(K):
        g_ref[pl.ds(i, 8, stride=K), :] = a_ref[i].T
    group_out[...] = g_ref[0:K, :]
    root_out[...] = g_ref[K : 2 * K, :]
    for departure in departures:
        departure.wait()


def last_call(group_sum, root_sum, factor, near, coupling_t):
    whole = pl.BlockSpec(memory_space=pltpu.VMEM)
    anywhere = pl.BlockSpec(memory_space=pl.ANY)
    square = jax.ShapeDtypeStruct((K, K), F32)
    return pl.pallas_call(
        last_kernel,
        out_shape=(
            jax.ShapeDtypeStruct(near.shape, BF16),
            jax.ShapeDtypeStruct(coupling_t.shape, BF16),
            square,
            square,
            square,
        ),
        in_specs=[whole] * 3 + [anywhere] * 2,
        out_specs=(anywhere,) * 2 + (whole,) * 3,
        scratch_shapes=[
            pltpu.VMEM(near.shape, BF16),
            pltpu.VMEM(coupling_t.shape, BF16),
            pltpu.VMEM((8 * K, K), F32),
            pltpu.VMEM((K, K, 8), F32),
            pltpu.SemaphoreType.DMA((4,)),
        ],
        compiler_params=pltpu.CompilerParams(vmem_limit_bytes=VMEM_LIMIT),
    )(group_sum, root_sum, factor, near, coupling_t)


def per_device(
    points, leaf_basis, inner_transfer, device_transfer, vectors, near_index, near_count, far_index
):
    near, coupling_t, factor, group_sum, root_sum = upsweep_call(
        near_count,
        far_index.T,
        leaf_basis.T,
        inner_transfer.T,
        device_transfer,
        points,
        near_index.T,
        vectors,
    )
    near_product, coupling_t, device_factor, group_factor, root_factor = last_call(
        group_sum, root_sum, factor, near, coupling_t
    )
    return near_product, coupling_t.T, device_factor, group_factor, root_factor


def solution(mesh):
    rows = P(("group", "sub"), None)
    return jax.shard_map(
        per_device,
        mesh=mesh,
        in_specs=(
            P(None, ("group", "sub")),
            rows,
            rows,
            rows,
            rows,
            rows,
            P(("group", "sub")),
            rows,
        ),
        out_specs=(rows,) * 5,
        check_vma=False,
    )
```

```python
import math

import jax
import jax.numpy as jnp
from jax import lax
from jax.experimental import pallas as pl
from jax.experimental.pallas import tpu as pltpu
from jax.sharding import PartitionSpec as P

K = 64
PAIR = 2 * K
LAYER = 4
RAD = 7
NEAR = 12
FAR = 3
HALO = 8
OWN = 32
WIDE = OWN + 2 * HALO
EDGE = HALO * K
SLOTS = 40
SHORT_SQ = 0.09
LONG_SQ = 2.25
RATIO = LONG_SQ / SHORT_SQ
SCALE = math.sqrt(0.5 / LONG_SQ * math.log2(math.e))
OFF = -131072.0
VMEM_LIMIT = 60 << 20
F32 = jnp.float32
BF16 = jnp.bfloat16
MESH = pl.DeviceIdType.MESH
PLANE = 15
WINDOW = 7
COVER = 4
SUMS = PLANE + WINDOW + COVER
COPIES = SUMS + 6
INPUTS = 6
FIRST_PART = 10


def dot(a, b):
    return jnp.dot(a, b, preferred_element_type=F32)


def dot_nt(a, b):
    return lax.dot_general(a, b, (((1,), (1,)), ((), ())), preferred_element_type=F32)


def exact_dot(a, b):
    return jnp.dot(a, b, preferred_element_type=F32, precision=lax.Precision.HIGHEST)


def exact_dot_t(a, b):
    return lax.dot_general(
        a, b, (((0,), (0,)), ((), ())), preferred_element_type=F32, precision=lax.Precision.HIGHEST
    )


def split3(x):
    high = x.astype(BF16)
    rest = x - high.astype(F32)
    middle = rest.astype(BF16)
    low = (rest - middle.astype(F32)).astype(BF16)
    return high, middle, low


def dot_wide(x, exact):
    rows = x.shape[0]
    parts = dot(jnp.concatenate(split3(x), axis=0), exact)
    return parts[:rows] + (parts[rows : 2 * rows] + parts[2 * rows :])


def in_first_half(shape):
    return lax.broadcasted_iota(jnp.int32, shape, len(shape) - 1) < K


def high_low(doubled):
    high = doubled.astype(BF16).astype(F32)
    return jnp.where(in_first_half(doubled.shape), high, doubled - high).astype(BF16)


def add_halves(x):
    return x + pltpu.roll(x, K, axis=1)


def cholesky_rows(a_ref, blocks, unroll=4):
    lanes = a_ref.shape[2]
    for block in blocks:
        first = 4 * block
        start = first // 8 * 8
        rows = tuple(a_ref[first + q, start:K, :] for q in range(4))

        def subtract(k, rows):
            done = a_ref[k, start:K, :]
            return tuple(
                rows[q] - a_ref[k, first + q : first + q + 1, :] * done for q in range(4)
            )

        if first:
            rows = lax.fori_loop(0, first, subtract, rows, unroll=unroll)
        rows = list(rows)
        index = lax.broadcasted_iota(jnp.int32, (K - start, lanes), 0)
        for q in range(4):
            at = first + q - start
            row = rows[q] * lax.rsqrt(rows[q][at : at + 1, :])
            row = jnp.where(index >= at, row, 0.0)
            a_ref[first + q, start:K, :] = row
            if start:
                a_ref[first + q, 0:start, :] = jnp.zeros((start, lanes), F32)
            for other in range(q + 1, 4):
                into = first + other - start
                rows[other] = rows[other] - row[into : into + 1, :] * row


def tree_gram(basis_ref, inner_ref, x_ref):
    last = inner_ref[:, 14 * PAIR : 15 * PAIR].astype(F32)
    path = [last[:, :K], last[:, K:]]
    for first, count in ((12, 4), (8, 8), (0, 16)):
        longer = []
        for m in range(count // 2):
            both = dot_wide(path[m], inner_ref[:, (first + m) * PAIR : (first + m + 1) * PAIR])
            longer += [both[:, :K], both[:, K:]]
        path = longer
    for m in range(16):
        x = dot_wide(path[m], basis_ref[:, m * PAIR : (m + 1) * PAIR])
        for part, value in enumerate(split3(x)):
            x_ref[part * K : (part + 1) * K, m * PAIR : (m + 1) * PAIR] = value
    parts = dot_nt(x_ref[0:PAIR, :], x_ref[...])
    parts = parts[:K] + parts[K:]
    low = parts[:, PAIR : PAIR + K]
    return (parts[:, :K] + parts[:, K:PAIR] + (low + low.T)) * (1.0 / OWN)


def unpack(ref):
    return jnp.concatenate([ref[:, :K], ref[:, K:]], axis=0)


def kernel_values(exponent):
    return jnp.exp2(exponent * RATIO) + 0.5 * jnp.exp2(exponent)


def leaf_rows(ref, leaf, rows):
    return ref[pl.ds(pl.multiple_of(leaf * rows, rows), rows), :]


def leaf_grams(basis_ref, top, g_ref):
    first = in_first_half((K, PAIR))
    for m in range(OWN // 2):
        v = basis_ref[:, m * PAIR : (m + 1) * PAIR]
        zero = jnp.zeros_like(v)
        one_each = jnp.concatenate([jnp.where(first, v, zero), jnp.where(first, zero, v)], axis=0)
        g_ref[m * PAIR : (m + 1) * PAIR, :] = dot_nt(one_each, v)
    for t in range(OWN, SLOTS):
        g_ref[t * K : (t + 1) * K, :] = top


def to_lanes(g_ref, a_ref):
    count = a_ref.shape[2]
    for i in range(K):
        a_ref[i] = g_ref[pl.ds(i, count, stride=K), :].T


def factor_pairs(a_ref, d_ref, pairs_ref, own_pairs_ref):
    for i in range(K):
        row = a_ref[i]
        d_ref[pl.ds(i, SLOTS, stride=K), :] = jnp.concatenate([row, row], axis=0).T
    first = in_first_half((K, PAIR))
    for t in range(OWN):
        doubled = d_ref[t * K : (t + 1) * K, :]
        high = doubled.astype(BF16).astype(F32)
        low = doubled - high
        pair = jnp.where(first, high, low).astype(BF16)
        pairs_ref[EDGE + t * K : EDGE + (t + 1) * K, :] = pair
        own_pairs_ref[t * PAIR : t * PAIR + K, :] = pair
        own_pairs_ref[t * PAIR + K : (t + 1) * PAIR, :] = jnp.where(first, low, high).astype(BF16)


def place_points(
    first_leaf,
    coords_ref,
    near_ref,
    count_ref,
    source_ref,
    target_ref,
    source_t_ref,
    target_t_ref,
    doubled_ref,
):
    lanes = WIDE * K
    leaf = lax.broadcasted_iota(jnp.int32, (3, lanes), 1) // K
    axis = lax.broadcasted_iota(jnp.int32, (3, lanes), 0)
    corner = jnp.where(
        axis == 0, leaf % 2, jnp.where(axis == 1, leaf // 2 % 2, leaf // LAYER - WIDE // LAYER // 2)
    )
    u = (coords_ref[...] + corner.astype(F32)) * SCALE
    high, middle, low = (part.astype(F32) for part in split3(u))
    norms = [part.astype(F32) for part in split3(-jnp.sum(u * u, axis=0, keepdims=True))]
    ones = jnp.ones((3, lanes), F32)
    own = slice(EDGE, lanes - EDGE)
    for n, (a, b) in enumerate(
        (
            (high, high),
            (high, middle),
            (middle, high),
            (high, low),
            (low, high),
            (middle, middle),
        )
    ):
        target_ref[3 * n : 3 * n + 3, :] = 2.0 * a[:, own]
        source_ref[3 * n : 3 * n + 3, :] = b
    target_ref[18:21, :] = ones[:, own]
    source_ref[21:24, :] = ones
    for n, part in enumerate(norms):
        source_ref[18 + n : 19 + n, :] = part
        target_ref[21 + n : 22 + n, :] = part[:, own]
    source_ref[24:32, :] = jnp.zeros((8, lanes), F32)

    slot = lax.broadcasted_iota(jnp.int32, (NEAR, OWN), 0)
    target = lax.broadcasted_iota(jnp.int32, (NEAR, OWN), 1)
    used = jnp.zeros((NEAR, OWN), jnp.int32)
    for t in range(OWN):
        used = jnp.where(target == t, count_ref[t], used)
    place = near_ref[...] - (first_leaf - LAYER) - target // LAYER * LAYER
    place = jnp.where(slot < used, place, -1)
    window = lax.broadcasted_iota(jnp.int32, (16, OWN), 0)
    bias = jnp.full((16, OWN), OFF, F32)
    for n in range(NEAR):
        bias = jnp.where(place[n : n + 1, :] == window, 0.0, bias)
    spread = lax.broadcasted_iota(jnp.int32, (OWN, OWN * K), 1) // K
    spread = (spread == lax.broadcasted_iota(jnp.int32, (OWN, OWN * K), 0)).astype(F32)
    target_ref[24:40, :] = dot(bias.astype(BF16), spread.astype(BF16))

    target_t_ref[...] = target_ref[...].T.astype(BF16)
    source_t_ref[...] = source_ref[...].T.astype(BF16)
    for t in range(OWN):
        one = target_ref[0:32, t * K : (t + 1) * K]
        doubled_ref[t] = jnp.concatenate([one, one], axis=1).astype(BF16)


def near_layers(layers, source_ref, target_t_ref, vectors_ref, near_out):
    width = LAYER * K
    window = lax.broadcasted_iota(jnp.int32, (16, width), 0)
    column = lax.broadcasted_iota(jnp.int32, (16, width), 1) // K
    for layer in layers:
        total = jnp.zeros((width, vectors_ref.shape[1]), F32)
        for step in range(3):
            at = (layer + 1 + step) * width
            place = (window == column + LAYER * step).astype(F32)
            source = jnp.concatenate([source_ref[0:24, at : at + width], place], axis=0)
            exponent = dot(
                target_t_ref[layer * width : (layer + 1) * width, :], source.astype(BF16)
            )
            weights = kernel_values(exponent).astype(BF16)
            rows = (layer + step) * width
            total = total + dot(weights, vectors_ref[rows : rows + width, :])
        near_out[layer * width : (layer + 1) * width, :] = total.astype(BF16)


def far_leaves(layer, p, at_start, at_end):
    places = []
    for k in range(FAR):
        shift = p - RAD + k + (12 if k + p >= FAR else 0)
        before = max(0, (3 - shift) // 4)
        beyond = max(0, shift // 4)
        place = LAYER * layer + shift
        if before:
            place = place + 15 * at_start * ((7 + before - layer) // 8)
        if beyond:
            place = place - 15 * at_end * ((layer + beyond) // 8)
        places.append(place)
    if isinstance(layer, int):
        places += list(range(11, 15)) if layer == 0 else list(range(17, 21))
    return places


def far_picks(read, names, first_leaf, places):
    values = [read(place + HALO) for place in places]
    picks = []
    for name in names:
        pick = values[0]
        for place, value in zip(places[1:], values[1:]):
            pick = lax.select(name == first_leaf + place, value, pick)
        picks.append(pick)
    return picks


def each_layer(run):
    last = OWN // LAYER - 1
    run(0)

    def step(layer, _):
        run(layer)
        return 0

    lax.fori_loop(1, last, step, 0, unroll=2)
    run(last)


def far_blocks(first_leaf, ends, far_ref, source_t_ref, doubled_ref, block_ref):
    def run(layer):
        for p in range(LAYER):
            t = LAYER * layer + p
            names = [far_ref[f, t] for f in range(FAR)]
            sources = far_picks(
                lambda leaf: leaf_rows(source_t_ref, leaf, K),
                names,
                first_leaf,
                far_leaves(layer, p, *ends),
            )
            exponent = dot(jnp.concatenate(sources, axis=0), doubled_ref[t])
            block_ref[t] = high_low(kernel_values(exponent))

    each_layer(run)


def far_halves(block_ref, own_pairs_ref, half_ref):
    def halves(t, _):
        value = dot_nt(block_ref[t], leaf_rows(own_pairs_ref, t, PAIR))
        half_ref[t] = high_low(add_halves(value) * (1.0 / K))
        return 0

    lax.fori_loop(0, OWN, halves, 0, unroll=4)


def far_products(first_leaf, ends, far_ref, half_ref, pairs_ref, coupling_out):
    def run(layer):
        values = []
        for p in range(LAYER):
            t = LAYER * layer + p
            names = [far_ref[f, t] for f in range(FAR)]
            factors = far_picks(
                lambda leaf: leaf_rows(pairs_ref, leaf, K),
                names,
                first_leaf,
                far_leaves(layer, p, *ends),
            )
            for f in range(FAR):
                half = half_ref[t, f * K : (f + 1) * K, :]
                values.append(add_halves(dot(factors[f], jnp.concatenate([half, half], axis=0))))
        first = in_first_half((K, PAIR))
        both = [jnp.where(first, values[2 * n], values[2 * n + 1]) for n in range(2 * FAR)]
        at = pl.multiple_of(layer * 2 * FAR * PAIR, PAIR)
        coupling_out[:, pl.ds(at, 2 * FAR * PAIR)] = jnp.concatenate(both, axis=1).astype(BF16)

    each_layer(run)


def turned(index, stride, size, by):
    at = lax.rem(index // stride, size)
    return index + (lax.rem(at + by, size) - at) * stride


def upsweep_kernel(
    count_ref,
    far_ref,
    basis_hbm,
    inner_hbm,
    transfer_hbm,
    points_hbm,
    near_hbm,
    vectors_hbm,
    near_hbm_out,
    coupling_hbm_out,
    factor_out,
    group_sum_out,
    root_sum_out,
    near_out,
    coupling_out,
    basis_ref,
    inner_ref,
    transfer_ref,
    near_ref,
    coords_ref,
    vectors_ref,
    g_ref,
    d_ref,
    a_ref,
    x_ref,
    pairs_ref,
    own_pairs_ref,
    source_ref,
    target_ref,
    source_t_ref,
    target_t_ref,
    doubled_ref,
    block_ref,
    half_ref,
    sum_ref,
    got_ref,
    in_sem,
    out_sem,
    send_sem,
    recv_sem,
):
    groups, subs = lax.axis_size("group"), lax.axis_size("sub")
    g, s = lax.axis_index("group"), lax.axis_index("sub")
    me = g * subs + s
    first_leaf = me * OWN
    count = groups * subs
    ends = ((count - me) // count, (me + 1) // count)
    after = lax.rem(me + 1, groups * subs)
    before = lax.rem(me + groups * subs - 1, groups * subs)
    after = (after // subs, lax.rem(after, subs))
    before = (before // subs, lax.rem(before, subs))

    hops = [(x, y) for x in (2, 1, 3, 0) for y in (2, 1, 3, 0) if x or y]
    hops = sorted(hops, key=lambda hop: -sum(min(h, 4 - h) for h in hop))
    plane = [(g, turned(turned(s, 2, 4, x), 8, 4, y)) for x, y in hops]
    steps = [(core, z) for z in (2, 1, 15, 0) for core in (1, 0) if core or z]
    window = [(turned(g, 1, 16, 16 - z), turned(s, 1, 2, core)) for core, z in steps]
    senders = [(turned(g, 1, 16, z), turned(s, 1, 2, core)) for core, z in steps]
    cover = [(turned(g, 1, 16, z), s) for z in (6, 10, 2, 14)]

    barrier = pltpu.get_barrier_semaphore()
    greeted = cover + senders + plane + [after, before]
    for device in greeted:
        pl.semaphore_signal(barrier, inc=1, device_id=device, device_id_type=MESH)

    lanes, rows = points_hbm.shape[1], vectors_hbm.shape[0]
    loads = [
        pltpu.make_async_copy(source, target, in_sem.at[n])
        for n, (source, target) in enumerate(
            (
                (inner_hbm, inner_ref),
                (basis_hbm, basis_ref),
                (transfer_hbm, transfer_ref),
                (points_hbm, coords_ref.at[:, EDGE : EDGE + lanes]),
                (near_hbm, near_ref),
                (vectors_hbm, vectors_ref.at[LAYER * K : LAYER * K + rows]),
            )
        )
    ]
    for load in loads:
        load.start()
    for load in loads[:3]:
        load.wait()

    top = tree_gram(basis_ref, inner_ref, x_ref)
    transfer = transfer_ref[...]
    gram = exact_dot_t(transfer, exact_dot(top, transfer))
    sum_ref[0] = jnp.concatenate([gram[: K // 2], gram[K // 2 :]], axis=1)

    leaf_grams(basis_ref, top, g_ref)
    to_lanes(g_ref, a_ref)
    cholesky_rows(a_ref, range(0, FIRST_PART))

    pl.semaphore_wait(barrier, len(greeted))

    def copy(number, source, target, device):
        return pltpu.make_async_remote_copy(
            src_ref=source,
            dst_ref=target,
            send_sem=send_sem.at[number],
            recv_sem=recv_sem.at[number],
            device_id=device,
            device_id_type=MESH,
        )

    def send(stage, first, devices):
        copies = [
            copy(first + n, sum_ref.at[stage], got_ref.at[first + n], device)
            for n, device in enumerate(devices)
        ]
        for one in copies:
            one.start()
        return copies

    def gather(total, first, copies):
        for n, one in enumerate(copies):
            one.wait()
            total = total + got_ref[first + n]
        return total

    sent = send(0, 0, plane)
    for load in loads[3:]:
        load.wait()
    halos = [
        copy(SUMS, coords_ref.at[:, lanes : lanes + EDGE], coords_ref.at[:, 0:EDGE], after),
        copy(
            SUMS + 1,
            coords_ref.at[:, EDGE : 2 * EDGE],
            coords_ref.at[:, EDGE + lanes : 2 * EDGE + lanes],
            before,
        ),
        copy(
            SUMS + 2,
            vectors_ref.at[rows : rows + LAYER * K],
            vectors_ref.at[0 : LAYER * K],
            after,
        ),
        copy(
            SUMS + 3,
            vectors_ref.at[LAYER * K : 2 * LAYER * K],
            vectors_ref.at[rows + LAYER * K : rows + 2 * LAYER * K],
            before,
        ),
    ]
    for halo in halos:
        halo.start()

    cholesky_rows(a_ref, range(FIRST_PART, 16))
    factor_pairs(a_ref, d_ref, pairs_ref, own_pairs_ref)
    edges = [
        copy(SUMS + 4, pairs_ref.at[OWN * K : OWN * K + EDGE], pairs_ref.at[0:EDGE], after),
        copy(
            SUMS + 5,
            pairs_ref.at[EDGE : 2 * EDGE],
            pairs_ref.at[OWN * K + EDGE : OWN * K + 2 * EDGE],
            before,
        ),
    ]
    for edge in edges:
        edge.start()
    factor_out[...] = exact_dot(d_ref[OWN * K : (OWN + 1) * K, 0:K], transfer)

    for halo in halos[:2]:
        halo.wait()
    place_points(
        first_leaf,
        coords_ref,
        near_ref,
        count_ref,
        source_ref,
        target_ref,
        source_t_ref,
        target_t_ref,
        doubled_ref,
    )
    near_layers(range(1, 5), source_ref, target_t_ref, vectors_ref, near_out)
    sum_ref[1] = gather(sum_ref[0], 0, sent)
    sent = send(1, PLANE, window)
    far_blocks(first_leaf, ends, far_ref, source_t_ref, doubled_ref, block_ref)
    near_layers(range(5, 7), source_ref, target_t_ref, vectors_ref, near_out)
    sum_ref[2] = gather(sum_ref[1], PLANE, sent)
    group_sum_out[...] = sum_ref[1] + got_ref[PLANE + steps.index((1, 0))]
    sent = send(2, PLANE + WINDOW, cover)
    for halo in halos[2:]:
        halo.wait()
    near_layers((0, 7), source_ref, target_t_ref, vectors_ref, near_out)
    near_move = pltpu.make_async_copy(near_out, near_hbm_out, out_sem.at[0])
    near_move.start()
    far_halves(block_ref, own_pairs_ref, half_ref)
    for edge in edges:
        edge.wait()
    far_products(first_leaf, ends, far_ref, half_ref, pairs_ref, coupling_out)
    coupling_move = pltpu.make_async_copy(coupling_out, coupling_hbm_out, out_sem.at[1])
    coupling_move.start()
    root_sum_out[...] = gather(jnp.zeros((K // 2, PAIR), F32), PLANE + WINDOW, sent)
    near_move.wait()
    coupling_move.wait()


def upsweep_call(near_count, far_t, basis_t, inner_t, transfer, points, near_t, vectors):
    whole = pl.BlockSpec(memory_space=pltpu.VMEM)
    scalars = pl.BlockSpec(memory_space=pltpu.SMEM)
    anywhere = pl.BlockSpec(memory_space=pltpu.HBM)
    packed = jax.ShapeDtypeStruct((K // 2, PAIR), F32)
    rows, columns = vectors.shape
    return pl.pallas_call(
        upsweep_kernel,
        out_shape=(
            jax.ShapeDtypeStruct(vectors.shape, BF16),
            jax.ShapeDtypeStruct((K, FAR * OWN * K), BF16),
            jax.ShapeDtypeStruct((K, K), F32),
            packed,
            packed,
        ),
        in_specs=[scalars] * 2 + [anywhere] * INPUTS,
        out_specs=(anywhere,) * 2 + (whole,) * 3,
        scratch_shapes=[
            pltpu.VMEM(vectors.shape, BF16),
            pltpu.VMEM((K, FAR * OWN * K), BF16),
            pltpu.VMEM(basis_t.shape, BF16),
            pltpu.VMEM(inner_t.shape, BF16),
            pltpu.VMEM((K, K), F32),
            pltpu.VMEM(near_t.shape, jnp.int32),
            pltpu.VMEM((3, WIDE * K), F32),
            pltpu.VMEM((rows + 2 * LAYER * K, columns), BF16),
            pltpu.VMEM((SLOTS * K, K), F32),
            pltpu.VMEM((SLOTS * K, PAIR), F32),
            pltpu.VMEM((K, K, SLOTS), F32),
            pltpu.VMEM((3 * K, OWN * K), BF16),
            pltpu.VMEM((WIDE * K, PAIR), BF16),
            pltpu.VMEM((OWN * PAIR, PAIR), BF16),
            pltpu.VMEM((32, WIDE * K), F32),
            pltpu.VMEM((40, OWN * K), F32),
            pltpu.VMEM((WIDE * K, 32), BF16),
            pltpu.VMEM((OWN * K, 40), BF16),
            pltpu.VMEM((OWN, 32, PAIR), BF16),
            pltpu.VMEM((OWN, FAR * K, PAIR), BF16),
            pltpu.VMEM((OWN, FAR * K, PAIR), BF16),
            pltpu.VMEM((3, K // 2, PAIR), F32),
            pltpu.VMEM((SUMS, K // 2, PAIR), F32),
            pltpu.SemaphoreType.DMA((INPUTS,)),
            pltpu.SemaphoreType.DMA((2,)),
            pltpu.SemaphoreType.DMA((COPIES,)),
            pltpu.SemaphoreType.DMA((COPIES,)),
        ],
        compiler_params=pltpu.CompilerParams(
            collective_id=0, has_side_effects=True, vmem_limit_bytes=VMEM_LIMIT
        ),
    )(near_count, far_t, basis_t, inner_t, transfer, points, near_t, vectors)


def unpack(ref):
    return jnp.concatenate([ref[:, :K], ref[:, K:]], axis=0)


def last_kernel(
    group_sum,
    root_sum,
    factor_ref,
    near_ref,
    coupling_ref,
    near_out,
    coupling_out,
    factor_out,
    group_out,
    root_out,
    near_buffer,
    coupling_buffer,
    g_ref,
    a_ref,
    sem,
):
    arrivals = [
        pltpu.make_async_copy(near_ref, near_buffer, sem.at[0]),
        pltpu.make_async_copy(coupling_ref, coupling_buffer, sem.at[1]),
    ]
    departures = [
        pltpu.make_async_copy(near_buffer, near_out, sem.at[2]),
        pltpu.make_async_copy(coupling_buffer, coupling_out, sem.at[3]),
    ]
    for arrival in arrivals:
        arrival.start()
    groups, subs = lax.axis_size("group"), lax.axis_size("sub")
    factor_out[...] = factor_ref[...]
    group = unpack(group_sum[...]) * (1.0 / subs)
    root = unpack(root_sum[...]) * (1.0 / (subs * groups))
    for n in range(8):
        g_ref[n * K : (n + 1) * K, :] = root if n else group
    to_lanes(g_ref, a_ref)
    cholesky_rows(a_ref, range(8), unroll=True)
    for arrival, departure in zip(arrivals, departures):
        arrival.wait()
        departure.start()
    cholesky_rows(a_ref, range(8, 16), unroll=True)
    for i in range(K):
        g_ref[pl.ds(i, 8, stride=K), :] = a_ref[i].T
    group_out[...] = g_ref[0:K, :]
    root_out[...] = g_ref[K : 2 * K, :]
    for departure in departures:
        departure.wait()


def last_call(group_sum, root_sum, factor, near, coupling_t):
    whole = pl.BlockSpec(memory_space=pltpu.VMEM)
    anywhere = pl.BlockSpec(memory_space=pl.ANY)
    square = jax.ShapeDtypeStruct((K, K), F32)
    return pl.pallas_call(
        last_kernel,
        out_shape=(
            jax.ShapeDtypeStruct(near.shape, BF16),
            jax.ShapeDtypeStruct(coupling_t.shape, BF16),
            square,
            square,
            square,
        ),
        in_specs=[whole] * 3 + [anywhere] * 2,
        out_specs=(anywhere,) * 2 + (whole,) * 3,
        scratch_shapes=[
            pltpu.VMEM(near.shape, BF16),
            pltpu.VMEM(coupling_t.shape, BF16),
            pltpu.VMEM((8 * K, K), F32),
            pltpu.VMEM((K, K, 8), F32),
            pltpu.SemaphoreType.DMA((4,)),
        ],
        compiler_params=pltpu.CompilerParams(vmem_limit_bytes=VMEM_LIMIT),
    )(group_sum, root_sum, factor, near, coupling_t)


def per_device(
    points, leaf_basis, inner_transfer, device_transfer, vectors, near_index, near_count, far_index
):
    near, coupling_t, factor, group_sum, root_sum = upsweep_call(
        near_count,
        far_index.T,
        leaf_basis.T,
        inner_transfer.T,
        device_transfer,
        points,
        near_index.T,
        vectors,
    )
    near_product, coupling_t, device_factor, group_factor, root_factor = last_call(
        group_sum, root_sum, factor, near, coupling_t
    )
    return near_product, coupling_t.T, device_factor, group_factor, root_factor


def solution(mesh):
    rows = P(("group", "sub"), None)
    return jax.shard_map(
        per_device,
        mesh=mesh,
        in_specs=(
            P(None, ("group", "sub")),
            rows,
            rows,
            rows,
            rows,
            rows,
            P(("group", "sub")),
            rows,
        ),
        out_specs=(rows,) * 5,
        check_vma=False,
    )
```
